256 devices in a mesh: tx: 16 (over z, core), gx: 8 (over x, y_lo), gy: 2 (over y_hi).
Axes of the slice: x: 4, y: 4 (y_hi: 2, y_lo: 2; y = y_hi * 2 + y_lo), z: 8, core: 2. Of those that a mesh axis runs over, the one named last changes fastest.
Arguments:
- cond_h: float32 [128, 32, 128], P('gx', 'gy'), may hold values from 0.1 to 1.5
- cond_v: float32 [128, 32, 128], P('gx', 'gy'), may hold values from 0.1 to 1.5
- fwd_init: float32 [16, 6, 128, 32, 128], P('tx', None, 'gx', 'gy'), may hold values from -6 to 6
- adj_init: float32 [16, 6, 128, 32, 128], P('tx', None, 'gx', 'gy'), may hold values from -6 to 6
- observed: float32 [16, 4, 8, 2, 2, 32], P('tx', None, 'gx', 'gy'), may hold values from -6 to 6
- footprint: int32 [16, 8, 2], P('tx', 'gx', 'gy'), may hold values 0 or 1
- owner: int32 [8, 2, 16], P('gx', 'gy'), may hold values from 0 to 15, each once within a row
- rec_cells: int32 [8, 2, 32], P('gx', 'gy'), may hold values from 0 to 255
Outputs:
- owned_gradient: float32 [8, 16, 2, 1, 32, 128], P('gx', 'tx', None, None, 'gy')
- misfit: float32 [], replicated
The draws below stay inside these ranges and needn't reach their ends.
Inputs may be any that keep to these rules, and one draw needn't show every extreme that they name: `owner`: each tile's row is a permutation of 0 to 15. `rec_cells`: cell index x * 16 + y within the tile; receivers may share a cell. `footprint`: 1 where the group's gradient counts in the tile.
All inputs are finite; a program needn't handle non-finite values.
Results may differ from the reference program's by a relative error of at most 0.00028.
Values sent between devices are 32-bit elements; how exact they have to be, the bound alone decides.
No kernel may reach another device: no remote copies, remote signals or barrier semaphores. Data moves between devices by JAX's collectives and lax.ppermute only.
A program may use at most 64 MiB of HBM per device.

```python
import math
import jax
import jax.numpy as jnp
from jax import lax

CX = 16
CY = 16
NZ = 128
RPT = 32
STEPS = 4
ZREC = 32
GROUPS = 16
TILES_X = 8
TILES_Y = 2
NX = 128
NY = 32
XB = 1
N_TX = 16


def set_ends(values, stream_key, smallest, top_value):
    place = [jax.random.randint(jax.random.fold_in(stream_key, axis), (), 0, length) for axis, length in enumerate(values.shape)]
    widest = values.shape.index(max(values.shape))
    beside = place[:widest] + [(place[widest] + 1) % values.shape[widest]] + place[widest + 1:]
    return values.at[tuple(place)].set(smallest).at[tuple(beside)].set(top_value)


def block_levels(stream_key, shape, split, smallest, top_value):
    factor_of, own = 1.0, jax.random.fold_in(stream_key, 6)
    for dim, shards_of in split:
        steps = jnp.exp(jax.random.uniform(jax.random.fold_in(own, dim), (shards_of,), jnp.float32, smallest / len(split), top_value / len(split)))
        factor_of = factor_of * jnp.repeat(steps, shape[dim] // shards_of).reshape([-1 if axis == dim else 1 for axis in range(len(shape))])
    return factor_of


def normal_values(key, shape, width, bound, split=(), kind=jnp.bfloat16):
    factor_of = block_levels(key, shape, split, -0.22, 0.18) if split else 1.0
    drawn = jax.random.normal(key, shape, jnp.float32) * width * factor_of
    return jnp.minimum(jnp.maximum(drawn, -bound), bound).astype(kind)


def setup_inputs(seed: int = 0) -> dict:
    arg_keys = jax.random.split(jax.random.key(seed), 9)
    cond_h = jnp.clip(jnp.exp(math.log(1.5) - 2.7080502 * jax.random.uniform(arg_keys[0], (NX, NY, NZ), jnp.float32) ** block_levels(arg_keys[0], (NX, NY, NZ), ((0, 8), (1, 2)), -0.2, 0.2)), 0.1, 1.5)
    cond_v = jnp.clip(jnp.exp(math.log(1.5) - 2.7080502 * jax.random.uniform(arg_keys[1], (NX, NY, NZ), jnp.float32) ** block_levels(arg_keys[1], (NX, NY, NZ), ((0, 8), (1, 2)), -0.2, 0.2)), 0.1, 1.5)
    fwd_init = normal_values(arg_keys[2], (GROUPS, 6, NX, NY, NZ), 1.0, 6.0, ((0, 16), (2, 8), (3, 2)), jnp.float32)
    adj_init = normal_values(arg_keys[3], (GROUPS, 6, NX, NY, NZ), 1.0, 6.0, ((0, 16), (2, 8), (3, 2)), jnp.float32)
    observed = normal_values(arg_keys[4], (GROUPS, STEPS, TILES_X, TILES_Y, 2, RPT), 1.0, 6.0, ((0, 16), (2, 8), (3, 2)), jnp.float32)
    footprint = set_ends((jax.random.randint(arg_keys[5], (GROUPS, TILES_X, TILES_Y), 0, 4) < 3).astype(jnp.int32), jax.random.fold_in(arg_keys[5], 1), 0, 1)
    owner = jax.vmap(lambda own: jax.random.permutation(own, GROUPS))(jax.random.split(arg_keys[6], TILES_X * TILES_Y)).reshape((TILES_X, TILES_Y, GROUPS)).astype(jnp.int32)
    rec_cells = set_ends(jax.random.randint(arg_keys[7], (TILES_X, TILES_Y, RPT), 0, CX * CY), jax.random.fold_in(arg_keys[7], 1), 0, (CX * CY) - 1).astype(jnp.int32)
    return {"cond_h": cond_h, "cond_v": cond_v, "fwd_init": fwd_init, "adj_init": adj_init, "observed": observed, "footprint": footprint, "owner": owner, "rec_cells": rec_cells}


STEP_DT = 0.5


def coefficients(conduct):
    half_rate = 0.25 * conduct
    return (1.0 - half_rate) / (1.0 + half_rate), STEP_DT / (1.0 + half_rate)


def ahead_of(values, axis_num):
    extent = values.shape[axis_num]
    tail_plane = jnp.zeros_like(lax.slice_in_dim(values, 0, 1, axis=axis_num))
    return jnp.concatenate([lax.slice_in_dim(values, 1, extent, axis=axis_num), tail_plane], axis=axis_num)


def before(values, axis_num):
    extent = values.shape[axis_num]
    head_plane = jnp.zeros_like(lax.slice_in_dim(values, 0, 1, axis=axis_num))
    return jnp.concatenate([head_plane, lax.slice_in_dim(values, 0, extent - 1, axis=axis_num)], axis=axis_num)


def curl_ahead(field):
    comp_x, comp_y, comp_z = field[0], field[1], field[2]
    out_x = (ahead_of(comp_z, 1) - comp_z) - (ahead_of(comp_y, 2) - comp_y)
    out_y = (ahead_of(comp_x, 2) - comp_x) - (ahead_of(comp_z, 0) - comp_z)
    out_z = (ahead_of(comp_y, 0) - comp_y) - (ahead_of(comp_x, 1) - comp_x)
    return jnp.stack([out_x, out_y, out_z])


def curl_before(field):
    comp_x, comp_y, comp_z = field[0], field[1], field[2]
    out_x = (comp_z - before(comp_z, 1)) - (comp_y - before(comp_y, 2))
    out_y = (comp_x - before(comp_x, 2)) - (comp_z - before(comp_z, 0))
    out_z = (comp_y - before(comp_y, 0)) - (comp_x - before(comp_x, 1))
    return jnp.stack([out_x, out_y, out_z])


def reference(cond_h, cond_v, fwd_init, adj_init, observed, footprint, owner, rec_cells):
    decay_h, drive_h = coefficients(cond_h)
    decay_v, drive_v = coefficients(cond_v)
    decay = jnp.stack([decay_h, decay_h, decay_v])
    drive = jnp.stack([drive_h, drive_h, drive_v])
    cell_ids = jnp.arange(CX * CY, dtype=jnp.int32)
    onehot = (rec_cells[..., None] == cell_ids).astype(jnp.float32)
    highest = lax.Precision.HIGHEST

    def record(electric):
        planes = electric[0:2, :, :, ZREC].reshape(2, TILES_X, CX, TILES_Y, CY)
        planes = planes.transpose(0, 1, 3, 2, 4).reshape(2, TILES_X, TILES_Y, CX * CY)
        return jnp.einsum("cabk,abrk->abcr", planes, onehot, precision=highest)

    def inject(electric, residual):
        spread = jnp.einsum("abcr,abrk->cabk", residual, onehot, precision=highest)
        spread = spread.reshape(2, TILES_X, TILES_Y, CX, CY).transpose(0, 1, 3, 2, 4).reshape(2, NX, NY)
        return electric.at[0:2, :, :, ZREC].add(spread)

    def one_group(state_pair, inputs):
        summed_grad, misfit_sum = state_pair
        forward, adjoint, observe, tile_flags = inputs
        electric, magnetic = forward[0:3], forward[3:6]
        stored = []
        residuals = []
        for step_idx in range(STEPS):
            magnetic = magnetic - STEP_DT * curl_ahead(electric)
            electric = decay * electric + drive * curl_before(magnetic)
            stored.append(electric)
            residuals.append(record(electric) - observe[step_idx])
        local_misfit = jnp.float32(0.0)
        for step_idx in range(STEPS):
            local_misfit = local_misfit + 0.5 * jnp.sum(residuals[step_idx] * residuals[step_idx])
        adj_e, adj_h = adjoint[0:3], adjoint[3:6]
        grad_h = jnp.zeros((NX, NY, NZ), jnp.float32)
        grad_v = jnp.zeros((NX, NY, NZ), jnp.float32)
        for step_idx in reversed(range(STEPS)):
            adj_e = inject(adj_e, residuals[step_idx])
            adj_h = adj_h - STEP_DT * curl_ahead(adj_e)
            adj_e = decay * adj_e + drive * curl_before(adj_h)
            kept = stored[step_idx]
            grad_h = grad_h + adj_e[0] * kept[0] + adj_e[1] * kept[1]
            grad_v = grad_v + adj_e[2] * kept[2]
        tile_mask = jnp.repeat(jnp.repeat(tile_flags.astype(jnp.float32), CX, axis=0), CY, axis=1)[:, :, None]
        summed_grad = summed_grad + jnp.stack([grad_h, grad_v]) * tile_mask
        return (summed_grad, misfit_sum + local_misfit), None

    start = (jnp.zeros((2, NX, NY, NZ), jnp.float32), jnp.float32(0.0))
    (summed_grad, misfit), _ = lax.scan(one_group, start, (fwd_init, adj_init, observed, footprint))
    blocked = summed_grad.reshape(2, TILES_X, N_TX, XB, TILES_Y, CY, NZ).transpose(1, 4, 2, 0, 3, 5, 6)
    chosen = jnp.take_along_axis(blocked, owner[:, :, :, None, None, None, None].astype(jnp.int32), axis=2)
    owned_part = chosen.transpose(0, 2, 3, 4, 1, 5, 6).reshape(TILES_X, N_TX, 2, XB, NY, NZ)
    return owned_part, misfit
```

```python
import jax
import jax.numpy as jnp
from jax import lax
from jax.experimental import pallas as pl
from jax.experimental.pallas import tpu as pltpu
from jax.sharding import PartitionSpec as P

STEPS = 4
ZREC = 32
STEP_DT = 0.5
HALO = 4
CX = 16
CY = 16
NZ = 128
EX = CX + 2 * HALO
EY = CY + 2 * HALO
F32 = jnp.float32
HIGHEST = lax.Precision.HIGHEST

LOW = [(c, x) for c in range(6) for x in range(CX - HALO + (c == 3), CX)]
HIGH = [(c, x) for c in range(6) for x in range(HALO - (c in (0, 3, 4, 5)))]
LOW_COND = [(c, x) for c in (6, 7) for x in range(CX - HALO + 1, CX)]
HIGH_COND = [(c, x) for c in (6, 7) for x in range(HALO - 1)]
VMEM = pl.BlockSpec(memory_space=pltpu.VMEM)
SMEM = pl.BlockSpec(memory_space=pltpu.SMEM)


def shape(*dims):
    return jax.ShapeDtypeStruct(dims, F32)


def params():
    return pltpu.CompilerParams(vmem_limit_bytes=16 * 1024 * 1024)


def plane_of(refs, comp, x):
    return refs[0][0, comp, x] if comp < 6 else refs[comp - 5][x]


def pack_kernel(low, high, n_in, *refs):
    ins, (to_next, to_prev, to_side, side_next, side_prev) = refs[:n_in], refs[n_in:]
    second = lax.axis_index("gy") == 1
    comps = 6 + n_in - 1

    def edge(plane):
        return jnp.where(second, plane[0:HALO], plane[CY - HALO : CY])

    for k, (c, x) in enumerate(low):
        plane = plane_of(ins, c, x)
        to_next[k] = plane
        side_next[k] = edge(plane)
    for k, (c, x) in enumerate(high):
        plane = plane_of(ins, c, x)
        to_prev[k] = plane
        side_prev[k] = edge(plane)
    for c in range(comps):
        for x in range(CX):
            to_side[c, x] = edge(plane_of(ins, c, x))


def pack(low, high, *arrays):
    comps = 6 + len(arrays) - 1
    return pl.pallas_call(
        lambda *refs: pack_kernel(low, high, len(arrays), *refs),
        out_shape=[
            shape(len(low), CY, NZ),
            shape(len(high), CY, NZ),
            shape(comps, CX, HALO, NZ),
            shape(len(low), HALO, NZ),
            shape(len(high), HALO, NZ),
        ],
        in_specs=[VMEM] * len(arrays),
        out_specs=[VMEM] * 5,
        compiler_params=params(),
        name="pack",
    )(*arrays)


def exchange(to_next, to_prev, to_side, side_next, side_prev):
    size_x = lax.axis_size("gx")
    size_y = lax.axis_size("gy")

    def pairs(dx, swap):
        return [
            (x * size_y + y, (x + dx) * size_y + (1 - y if swap else y))
            for x in range(size_x)
            for y in range(size_y)
            if 0 <= x + dx < size_x
        ]

    both = ("gx", "gy")
    return (
        lax.ppermute(to_next, both, pairs(1, False)),
        lax.ppermute(to_prev, both, pairs(-1, False)),
        lax.ppermute(to_side, both, pairs(0, True)),
        lax.ppermute(side_next, both, pairs(1, True)),
        lax.ppermute(side_prev, both, pairs(-1, True)),
    )


def assemble(low, high, ins, halos, dest, first):
    from_prev, from_next, from_side, side_prev, side_next = halos
    zero_rows = jnp.zeros((HALO, NZ), F32)
    zero_plane = jnp.zeros((EY, NZ), F32)

    def put_side(ref, index, i, rows):
        ref[index, i, CY : CY + HALO] = jnp.where(first, rows, zero_rows)
        ref[index, i, CY + HALO : EY] = jnp.where(first, zero_rows, rows)

    comps = 6 + len(ins) - 1
    for c in range(comps):
        ref, index = dest(c)
        filled = set()
        for x in range(CX):
            ref[index, HALO + x, 0:CY] = plane_of(ins, c, x)
            put_side(ref, index, HALO + x, from_side[c, x])
            filled.add(HALO + x)
        for k, (comp, x) in enumerate(low):
            if comp == c:
                i = x - (CX - HALO)
                ref[index, i, 0:CY] = from_prev[k]
                put_side(ref, index, i, side_prev[k])
                filled.add(i)
        for k, (comp, x) in enumerate(high):
            if comp == c:
                i = x + HALO + CX
                ref[index, i, 0:CY] = from_next[k]
                put_side(ref, index, i, side_next[k])
                filled.add(i)
        for i in range(EX):
            if i not in filled:
                ref[index, i] = zero_plane


def helpers(gy):
    lane = lax.broadcasted_iota(jnp.int32, (EY, NZ), 1)
    row = lax.broadcasted_iota(jnp.int32, (EY, NZ), 0)
    y = jnp.where(row < CY + HALO, row, row - EY) + gy * CY
    inside = (y >= 0) & (y < 2 * CY)
    last, start = lane == NZ - 1, lane == 0

    def z_up(f):
        return jnp.where(last, 0.0, pltpu.roll(f, NZ - 1, 1))

    def z_down(f):
        return jnp.where(start, 0.0, pltpu.roll(f, 1, 1))

    def y_up(f):
        return pltpu.roll(f, EY - 1, 0)

    def y_down(f):
        return pltpu.roll(f, 1, 0)

    return lane, inside, z_up, z_down, y_up, y_down


def in_grid(gx, i):
    x = gx * CX + i - HALO
    return (x >= 0) & (x < 8 * CX)


def sweep(step, gx, elec, mag, coef, tools, load):
    _, inside, z_up, z_down, y_up, y_down = tools
    half = jnp.where(inside, STEP_DT, 0.0)
    zero = jnp.zeros((EY, NZ), F32)

    def body(i, carry):
        ex, ey, ez, hy_before, hz_before = carry
        ex_next, ey_next, ez_next = load(i + 1)
        rate = jnp.where(in_grid(gx, i), half, zero)
        hx = mag[0, i] - rate * ((y_up(ez) - ez) - (z_up(ey) - ey))
        hy = mag[1, i] - rate * ((z_up(ex) - ex) - (ez_next - ez))
        hz = mag[2, i] - rate * ((ey_next - ey) - (y_up(ex) - ex))
        mag[0, i] = hx
        mag[1, i] = hy
        mag[2, i] = hz
        decay_h, drive_h, decay_v, drive_v = (coef[k, i] for k in range(4))
        elec[0, i] = decay_h * ex + drive_h * ((hz - y_down(hz)) - (hy - z_down(hy)))
        elec[1, i] = decay_h * ey + drive_h * ((hx - z_down(hx)) - (hz - hz_before))
        elec[2, i] = decay_v * ez + drive_v * ((hy - hy_before) - (hx - y_down(hx)))
        return (ex_next, ey_next, ez_next, hy, hz)

    lax.fori_loop(step, EX - 1 - step, body, (*load(step), zero, zero))


def forward_kernel(fwd, cond_h, cond_v, *refs):
    halos, refs = refs[:5], refs[5:]
    observed, rec_vec, rec, coef, stored, spread, block, elec, mag, rows = refs
    gx, gy = lax.axis_index("gx"), lax.axis_index("gy")
    tools = helpers(gy)
    lane, inside = tools[0], tools[1]

    def dest(c):
        return ((elec, c) if c < 3 else (mag, c - 3)) if c < 6 else (coef, 2 * (c - 6))

    assemble(LOW + LOW_COND, HIGH + HIGH_COND, (fwd, cond_h, cond_v), halos, dest, gy == 0)

    def coefficients(i, carry):
        keep = inside & in_grid(gx, i)
        for k in (0, 2):
            half_rate = 0.25 * coef[k, i]
            coef[k, i] = jnp.where(keep, (1.0 - half_rate) / (1.0 + half_rate), 0.0)
            coef[k + 1, i] = jnp.where(keep, STEP_DT / (1.0 + half_rate), 0.0)
        return carry

    lax.fori_loop(0, EX, coefficients, 0)

    def load(i):
        return elec[0, i], elec[1, i], elec[2, i]

    for step in range(STEPS):
        sweep(step, gx, elec, mag, coef, tools, load)
        stored[step] = elec[:, HALO : HALO + CX, 0:CY]

    for r in range(rec.shape[0]):
        x, y = rec[r] // CY, rec[r] % CY
        for step in range(STEPS):
            for c in range(2):
                rows[pl.ds((2 * step + c) * 32 + r, 1), :] = stored[step, c, x, pl.ds(y, 1), :]
    pick = (lax.broadcasted_iota(jnp.int32, (8, NZ), 1) == ZREC).astype(F32)
    picked = lax.dot_general(
        pick, rows[...], (((1,), (1,)), ((), ())), precision=HIGHEST, preferred_element_type=F32
    )
    lane8 = lax.broadcasted_iota(jnp.int32, (8, NZ), 1)
    row8 = lax.broadcasted_iota(jnp.int32, (8, NZ), 0)
    own = jnp.where(lane8 // 32 == row8, picked[:, 0:NZ], 0.0)
    own = own + jnp.where(lane8 // 32 + 4 == row8, picked[:, NZ : 2 * NZ], 0.0)
    own = own + pltpu.roll(own, 64, 1)
    own = own + pltpu.roll(own, 32, 1)
    residual = own[:, 0:32] - observed[...]
    misfit = 0.5 * jnp.sum(residual * residual)
    cells = rec_vec[...]
    at_y = (cells % CY == lax.broadcasted_iota(jnp.int32, (CY, 32), 0)).astype(F32)
    at_x = cells // CY == lax.broadcasted_iota(jnp.int32, (NZ, 32), 0) // 8
    weighted = jnp.where(at_x, jnp.tile(residual, (16, 1)), 0.0)
    spread_now = lax.dot_general(
        at_y, weighted, (((1,), (1,)), ((), ())), precision=HIGHEST, preferred_element_type=F32
    )
    spread[...] = spread_now
    low_rows, high_rows = spread_now[0:8], spread_now[8:16]
    edges = jnp.where((lane8 < 32) | (lane8 >= 96), low_rows, pltpu.roll(high_rows, 64, 1))
    is_first = gy == 0
    side = jnp.where(is_first, high_rows, low_rows)
    used = row8 // HALO == 1 - gy
    side = jnp.where(used, side, misfit)
    for t in range(16):
        block[t, 0:8] = edges
        block[t, 8:16] = side


def adjoint_kernel(adj, *refs):
    halos, refs = refs[:5], refs[5:]
    coef, stored, spread, blocks, foot, owner, out, elec, mag, inject, grad = refs
    gx, gy = lax.axis_index("gx"), lax.axis_index("gy")
    tools = helpers(gy)
    lane, inside = tools[0], tools[1]

    def dest(c):
        return (elec, c) if c < 3 else (mag, c - 3)

    assemble(LOW, HIGH, (adj,), halos, dest, gy == 0)

    row8 = lax.broadcasted_iota(jnp.int32, (8, NZ), 0)
    used = row8 // HALO == gy
    for k, dx in enumerate((-1, 0, 1)):
        there = (gx + dx >= 0) & (gx + dx < 8)
        near = jnp.clip(gx + dx, 0, 7)
        if dx == 0:
            inject[k, 0:16] = spread[...]
        else:
            edges = jnp.where(there, blocks[2 * near + gy, 0:8], 0.0)
            inject[k, 0:8] = edges
            inject[k, 8:16] = pltpu.roll(edges, 64, 1)
        side = blocks[2 * near + 1 - gy, 8:16]
        inject[k, 16:24] = jnp.where(used & there, side, 0.0)

    at_depth = lane == ZREC

    for step in range(STEPS):
        when = STEPS - 1 - step

        def load(i, when=when):
            tile = jnp.where(i < HALO, 0, jnp.where(i < HALO + CX, 1, 2))
            x = (i + CX - HALO) % CX
            source = inject[tile]
            shift = (ZREC + NZ - (x * 8 + 2 * when)) % NZ
            add_x = jnp.where(at_depth, pltpu.roll(source, shift, 1), 0.0)
            add_y = jnp.where(at_depth, pltpu.roll(source, (shift + NZ - 1) % NZ, 1), 0.0)
            return elec[0, i] + add_x, elec[1, i] + add_y, elec[2, i]

        sweep(step, gx, elec, mag, coef, tools, load)

        def accumulate(x, carry, when=when, step=step):
            ax, ay, az = (elec[c, HALO + x, 0:CY] for c in range(3))
            horizontal = ax * stored[when, 0, x] + ay * stored[when, 1, x]
            vertical = az * stored[when, 2, x]
            if step:
                horizontal = grad[0, x] + horizontal
                vertical = grad[1, x] + vertical
            grad[0, x] = horizontal
            grad[1, x] = vertical
            return carry

        lax.fori_loop(0, CX, accumulate, 0)

    flag = foot[0].astype(F32)
    misfit = blocks[0, 8:16][0:1]
    for t in range(1, 16):
        top = 0 if t % 2 == 0 else HALO
        misfit = misfit + blocks[t, 8:16][top : top + 1]
    misfit = jnp.broadcast_to(misfit, (8, NZ))
    for t in range(16):
        out[t, 0:16] = grad[0, owner[t]] * flag
        out[t, 16:32] = grad[1, owner[t]] * flag
        out[t, 32:40] = misfit


def sum_kernel(blocks, part, misfit):
    total = blocks[0]
    for t in range(1, 16):
        total = total + blocks[t]
    part[0, 0, 0, 0] = total[0:16]
    part[0, 0, 1, 0] = total[16:32]
    misfit[...] = total[32:33, 0:1]


def on_device(cond_h, cond_v, fwd_init, adj_init, observed, footprint, owner, rec_cells):
    sent = pack(LOW + LOW_COND, HIGH + HIGH_COND, fwd_init, cond_h, cond_v)
    adj_sent = pack(LOW, HIGH, adj_init)
    halos = exchange(*sent)
    adj_halos = exchange(*adj_sent)
    rec = rec_cells.reshape(32)
    coef, stored, spread, block = pl.pallas_call(
        forward_kernel,
        out_shape=[
            shape(4, EX, EY, NZ),
            shape(STEPS, 3, CX, CY, NZ),
            shape(CY, NZ),
            shape(16, 16, NZ),
        ],
        in_specs=[VMEM] * 10 + [SMEM],
        out_specs=[VMEM] * 4,
        scratch_shapes=[
            pltpu.VMEM((3, EX, EY, NZ), F32),
            pltpu.VMEM((3, EX, EY, NZ), F32),
            pltpu.VMEM((256, NZ), F32),
        ],
        compiler_params=params(),
        name="forward",
    )(fwd_init, cond_h, cond_v, *halos, observed.reshape(8, 32), rec.reshape(1, 32), rec)
    blocks = lax.all_to_all(block, ("gx", "gy"), 0, 0, tiled=True)
    ordered = pl.pallas_call(
        adjoint_kernel,
        out_shape=shape(16, 40, NZ),
        in_specs=[VMEM] * 10 + [SMEM, SMEM],
        out_specs=VMEM,
        scratch_shapes=[
            pltpu.VMEM((3, EX, EY, NZ), F32),
            pltpu.VMEM((3, EX, EY, NZ), F32),
            pltpu.VMEM((3, EY, NZ), F32),
            pltpu.VMEM((2, CX, CY, NZ), F32),
        ],
        compiler_params=params(),
        name="adjoint",
    )(
        adj_init,
        *adj_halos,
        coef,
        stored,
        spread,
        blocks,
        footprint.reshape(1),
        owner.reshape(16),
    )
    summed = lax.all_to_all(ordered, "tx", 0, 0, tiled=True)
    part, misfit = pl.pallas_call(
        sum_kernel,
        out_shape=[shape(1, 1, 2, 1, CY, NZ), shape(1, 1)],
        in_specs=[VMEM],
        out_specs=[VMEM, VMEM],
        compiler_params=params(),
        name="total",
    )(summed)
    return part, misfit.reshape(())


def solution(mesh):
    placed = (
        P("gx", "gy", None),
        P("gx", "gy", None),
        P("tx", None, "gx", "gy", None),
        P("tx", None, "gx", "gy", None),
        P("tx", None, "gx", "gy", None, None),
        P("tx", "gx", "gy"),
        P("gx", "gy", None),
        P("gx", "gy", None),
    )
    return jax.shard_map(
        on_device,
        mesh=mesh,
        in_specs=placed,
        out_specs=(P("gx", "tx", None, None, "gy", None), P()),
        check_vma=False,
    )
```

```python
import jax
import jax.numpy as jnp
from jax import lax
from jax.experimental import pallas as pl
from jax.experimental.pallas import tpu as pltpu
from jax.sharding import PartitionSpec as P

STEPS = 4
ZREC = 32
STEP_DT = 0.5
HALO = 4
CX = 16
CY = 16
NZ = 128
EX = CX + 2 * HALO
EXP = EX + 4
EY = CY + 2 * HALO
F32 = jnp.float32
HIGHEST = lax.Precision.HIGHEST

COMPS = 14
LOW = [
    (c, x)
    for c in range(COMPS)
    for x in range(CX - HALO + (c in (3, 6, 7, 11)), CX)
]
HIGH = [(c, x) for c in range(COMPS) for x in range(HALO - (c not in (1, 2, 9, 10)))]
VMEM = pl.BlockSpec(memory_space=pltpu.VMEM)
SMEM = pl.BlockSpec(memory_space=pltpu.SMEM)


def shape(*dims):
    return jax.ShapeDtypeStruct(dims, F32)


def params():
    return pltpu.CompilerParams(vmem_limit_bytes=8 * 1024 * 1024)


def plane_of(refs, comp, x):
    fwd, cond_h, cond_v, adj = refs
    if comp < 6:
        return fwd[0, comp, x]
    return adj[0, comp - 8, x] if comp > 7 else (cond_h, cond_v)[comp - 6][x]


def pack_kernel(fwd, cond_h, cond_v, adj, *refs):
    to_next, to_prev, to_side, side_next, side_prev = refs[:5]
    bufs, sem = refs[5:9], refs[9]
    copies = [
        pltpu.make_async_copy(src, dst, sem.at[k])
        for k, (src, dst) in enumerate(zip((fwd, cond_h, cond_v, adj), bufs))
    ]
    for copy in copies:
        copy.start()
    second = lax.axis_index("gy") == 1

    def edge(plane):
        return jnp.where(second, plane[0:HALO], plane[CY - HALO : CY])

    for which, comps in ((0, range(6)), (1, (6,)), (2, (7,)), (3, range(8, COMPS))):
        copies[which].wait()
        for c in comps:
            edges = [edge(plane_of(bufs, c, x)) for x in range(CX)]
            for x in range(CX):
                to_side[c, x] = edges[x]
            for k, (comp, x) in enumerate(LOW):
                if comp == c:
                    to_next[k] = plane_of(bufs, c, x)
                    side_next[k] = edges[x]
            for k, (comp, x) in enumerate(HIGH):
                if comp == c:
                    to_prev[k] = plane_of(bufs, c, x)
                    side_prev[k] = edges[x]


def pack(*arrays):
    return pl.pallas_call(
        pack_kernel,
        out_shape=[
            shape(len(LOW), CY, NZ),
            shape(len(HIGH), CY, NZ),
            shape(COMPS, CX, HALO, NZ),
            shape(len(LOW), HALO, NZ),
            shape(len(HIGH), HALO, NZ),
        ],
        in_specs=[pl.BlockSpec(memory_space=pltpu.HBM)] * 4,
        out_specs=[VMEM] * 5,
        scratch_shapes=[pltpu.VMEM(a.shape, F32) for a in arrays]
        + [pltpu.SemaphoreType.DMA((4,))],
        compiler_params=params(),
        name="pack",
    )(*arrays)


def exchange(to_next, to_prev, to_side, side_next, side_prev):
    size_x = lax.axis_size("gx")
    size_y = lax.axis_size("gy")

    def pairs(dx, swap):
        return [
            (x * size_y + y, (x + dx) * size_y + (1 - y if swap else y))
            for x in range(size_x)
            for y in range(size_y)
            if 0 <= x + dx < size_x
        ]

    both = ("gx", "gy")
    return (
        lax.ppermute(to_next, both, pairs(1, False)),
        lax.ppermute(to_prev, both, pairs(-1, False)),
        lax.ppermute(to_side, both, pairs(0, True)),
        lax.ppermute(side_next, both, pairs(1, True)),
        lax.ppermute(side_prev, both, pairs(-1, True)),
    )


def assemble(own, halos, comps, first):
    from_prev, from_next, from_side, side_prev, side_next = halos
    zero_rows = jnp.zeros((HALO, NZ), F32)
    zero_plane = jnp.zeros((EY, NZ), F32)

    def put(ref, index, i, plane, rows):
        ref[index, i, 0:CY] = plane
        ref[index, i, CY : CY + HALO] = jnp.where(first, rows, zero_rows)
        ref[index, i, CY + HALO : EY] = jnp.where(first, zero_rows, rows)

    for c, (ref, index) in comps.items():
        filled = set()
        for x in range(CX):
            put(ref, index, HALO + x, own(c, x), from_side[c, x])
            filled.add(HALO + x)
        for k, (comp, x) in enumerate(LOW):
            if comp == c:
                i = x - (CX - HALO)
                put(ref, index, i, from_prev[k], side_prev[k])
                filled.add(i)
        for k, (comp, x) in enumerate(HIGH):
            if comp == c:
                i = x + HALO + CX
                put(ref, index, i, from_next[k], side_next[k])
                filled.add(i)
        for i in range(EXP):
            if i not in filled:
                ref[index, i] = zero_plane


def helpers(gy):
    lane = lax.broadcasted_iota(jnp.int32, (EY, NZ), 1)
    row = lax.broadcasted_iota(jnp.int32, (EY, NZ), 0)
    y = jnp.where(row < CY + HALO, row, row - EY) + gy * CY
    inside = (y >= 0) & (y < 2 * CY)
    last, start = lane == NZ - 1, lane == 0

    def z_up(f):
        return jnp.where(last, 0.0, pltpu.roll(f, NZ - 1, 1))

    def z_down(f):
        return jnp.where(start, 0.0, pltpu.roll(f, 1, 1))

    def y_up(f):
        return pltpu.roll(f, EY - 1, 0)

    def y_down(f):
        return pltpu.roll(f, 1, 0)

    return lane, inside, z_up, z_down, y_up, y_down


def in_grid(gx, i):
    x = gx * CX + i - HALO
    return (x >= 0) & (x < 8 * CX)


MODE = "fused"
UNROLL = 8


def sweep(step, gx, elec, mag, coef, tools):
    _, inside, z_up, z_down, y_up, y_down = tools
    half = jnp.where(inside, STEP_DT, 0.0)
    zero = jnp.zeros((EY, NZ), F32)
    turns = -(-(EX - 1 - 2 * step) // UNROLL)

    def magnetic(i, field, after):
        ex, ey, ez = field
        _, ey_next, ez_next = after
        rate = jnp.where(in_grid(gx, i), half, zero)
        hx = mag[0, i] - rate * ((y_up(ez) - ez) - (z_up(ey) - ey))
        hy = mag[1, i] - rate * ((z_up(ex) - ex) - (ez_next - ez))
        hz = mag[2, i] - rate * ((ey_next - ey) - (y_up(ex) - ex))
        return hx, hy, hz

    def electric(i, field, now, before):
        ex, ey, ez = field
        hx, hy, hz = now
        decay_h, drive_h, decay_v, drive_v = (coef[k, i] for k in range(4))
        ex = decay_h * ex + drive_h * ((hz - y_down(hz)) - (hy - z_down(hy)))
        ey = decay_h * ey + drive_h * ((hx - z_down(hx)) - (hz - before[2]))
        ez = decay_v * ez + drive_v * ((hy - before[1]) - (hx - y_down(hx)))
        return ex, ey, ez

    def planes(ref, i, n):
        return [tuple(ref[c, i + k] for c in range(3)) for k in range(n)]

    def put(ref, i, values):
        for k, plane in enumerate(values):
            for c in range(3):
                ref[c, i + k] = plane[c]

    if MODE == "fused":

        def body(turn, carry):
            i = step + turn * UNROLL
            field = planes(elec, i, UNROLL + 1)
            now = [magnetic(i + k, field[k], field[k + 1]) for k in range(UNROLL)]
            put(mag, i, now)
            before = [(None, *carry)] + now[:-1]
            put(elec, i, [electric(i + k, field[k], now[k], before[k]) for k in range(UNROLL)])
            return now[-1][1:]

        lax.fori_loop(0, turns, body, (zero, zero))
    else:

        def body_h(turn, carry):
            i = step + turn * UNROLL
            field = planes(elec, i, UNROLL + 1)
            put(mag, i, [magnetic(i + k, field[k], field[k + 1]) for k in range(UNROLL)])
            return carry

        def body_e(turn, carry):
            i = step + 1 + turn * UNROLL
            field = planes(elec, i, UNROLL)
            now = planes(mag, i - 1, UNROLL + 1)
            put(elec, i, [electric(i + k, field[k], now[k + 1], now[k]) for k in range(UNROLL)])
            return carry

        lax.fori_loop(0, turns, body_h, 0)
        lax.fori_loop(0, -(-(EX - 2 - 2 * step) // UNROLL), body_e, 0)


def forward_kernel(fwd, cond_h, cond_v, *refs):
    halos, refs = refs[:5], refs[5:]
    observed, rec_vec, rec, coef, stored, spread, block, elec, mag, rows = refs
    gx, gy = lax.axis_index("gx"), lax.axis_index("gy")
    tools = helpers(gy)
    lane, inside = tools[0], tools[1]

    comps = {c: (elec, c) if c < 3 else (mag, c - 3) for c in range(6)}
    comps |= {6: (coef, 0), 7: (coef, 2)}
    assemble(lambda c, x: plane_of((fwd, cond_h, cond_v, None), c, x), halos, comps, gy == 0)

    def coefficients(i, carry):
        keep = inside & in_grid(gx, i)
        for k in (0, 2):
            half_rate = 0.25 * coef[k, i]
            inverse = 1.0 / (1.0 + half_rate)
            coef[k, i] = jnp.where(keep, (1.0 - half_rate) * inverse, 0.0)
            coef[k + 1, i] = jnp.where(keep, STEP_DT * inverse, 0.0)
        return carry

    lax.fori_loop(0, EX, coefficients, 0)
    for k in (1, 3):
        coef[k, EX:EXP] = jnp.zeros((EXP - EX, EY, NZ), F32)

    for step in range(STEPS):
        sweep(step, gx, elec, mag, coef, tools)
        stored[step] = elec[:, HALO : HALO + CX, 0:CY]

    for r in range(rec.shape[0]):
        x, y = rec[r] >> 4, rec[r] & 15
        for step in range(STEPS):
            for c in range(2):
                rows[pl.ds((2 * step + c) * 32 + r, 1), :] = stored[step, c, x, pl.ds(y, 1), :]
    pick = (lax.broadcasted_iota(jnp.int32, (8, NZ), 1) == ZREC).astype(F32)
    picked = lax.dot_general(
        pick, rows[...], (((1,), (1,)), ((), ())), precision=HIGHEST, preferred_element_type=F32
    )
    lane8 = lax.broadcasted_iota(jnp.int32, (8, NZ), 1)
    row8 = lax.broadcasted_iota(jnp.int32, (8, NZ), 0)
    own = jnp.where(lane8 // 32 == row8, picked[:, 0:NZ], 0.0)
    own = own + jnp.where(lane8 // 32 + 4 == row8, picked[:, NZ : 2 * NZ], 0.0)
    own = own + pltpu.roll(own, 64, 1)
    own = own + pltpu.roll(own, 32, 1)
    residual = own[:, 0:32] - observed[...]
    misfit = 0.5 * jnp.sum(residual * residual)
    cells = rec_vec[...]
    at_y = ((cells & 15) == lax.broadcasted_iota(jnp.int32, (CY, 32), 0)).astype(F32)
    at_x = (cells >> 4) == lax.broadcasted_iota(jnp.int32, (NZ, 32), 0) // 8
    weighted = jnp.where(at_x, jnp.tile(residual, (16, 1)), 0.0)
    spread_now = lax.dot_general(
        at_y, weighted, (((1,), (1,)), ((), ())), precision=HIGHEST, preferred_element_type=F32
    )
    spread[...] = spread_now
    low_rows, high_rows = spread_now[0:8], spread_now[8:16]
    edges = jnp.where((lane8 < 32) | (lane8 >= 96), low_rows, pltpu.roll(high_rows, 64, 1))
    is_first = gy == 0
    side = jnp.where(is_first, high_rows, low_rows)
    used = row8 // HALO == 1 - gy
    side = jnp.where(used, side, misfit)
    for t in range(16):
        block[t, 0:8] = edges
        block[t, 8:16] = side


def adjoint_kernel(adj, *refs):
    halos, refs = refs[:5], refs[5:]
    coef, stored, spread, blocks, foot, owner, keep, send, elec, mag, inject, grad = refs
    gx, gy = lax.axis_index("gx"), lax.axis_index("gy")
    tools = helpers(gy)
    lane, inside = tools[0], tools[1]

    comps = {8 + c: (elec, c) if c < 3 else (mag, c - 3) for c in range(6)}
    assemble(lambda c, x: adj[0, c - 8, x], halos, comps, gy == 0)

    row8 = lax.broadcasted_iota(jnp.int32, (8, NZ), 0)
    used = row8 // HALO == gy
    for k, dx in enumerate((-1, 0, 1)):
        there = (gx + dx >= 0) & (gx + dx < 8)
        near = jnp.clip(gx + dx, 0, 7)
        if dx == 0:
            inject[k, 0:16] = spread[...]
        else:
            edges = jnp.where(there, blocks[2 * near + gy, 0:8], 0.0)
            inject[k, 0:8] = edges
            inject[k, 8:16] = pltpu.roll(edges, 64, 1)
        side = blocks[2 * near + 1 - gy, 8:16]
        inject[k, 16:24] = jnp.where(used & there, side, 0.0)

    at_depth = lane == ZREC

    for step in range(STEPS):
        when = STEPS - 1 - step

        def add(turn, carry, when=when):
            for k in range(4):
                i = turn * 4 + k
                tile = jnp.where(turn == 0, 0, jnp.where(turn < 5, 1, 2))
                x = (i + CX - HALO) & (CX - 1)
                source = inject[tile]
                shift = (ZREC + NZ - (x * 8 + 2 * when)) & (NZ - 1)
                for c in range(2):
                    moved = pltpu.roll(source, (shift - c) & (NZ - 1), 1)
                    elec[c, i] += jnp.where(at_depth, moved, 0.0)
            return carry

        lax.fori_loop(0, EX // 4, add, 0)
        sweep(step, gx, elec, mag, coef, tools)

        def accumulate(x, carry, when=when, step=step):
            ax, ay, az = (elec[c, HALO + x, 0:CY] for c in range(3))
            horizontal = ax * stored[when, 0, x] + ay * stored[when, 1, x]
            vertical = az * stored[when, 2, x]
            if step:
                horizontal = grad[0, x] + horizontal
                vertical = grad[1, x] + vertical
            grad[0, x] = horizontal
            grad[1, x] = vertical
            return carry

        lax.fori_loop(0, CX, accumulate, 0)

    flag = foot[0].astype(F32)
    misfit = blocks[0, 8:16][0:1]
    for t in range(1, 16):
        top = 0 if t % 2 == 0 else HALO
        misfit = misfit + blocks[t, 8:16][top : top + 1]
    core = lax.axis_index("tx") & 1
    for z in range(8):
        for ref, mine in ((keep, core), (send, 1 - core)):
            row = owner[2 * z + mine]
            ref[32 * z : 32 * z + 16] = grad[0, row] * flag
            ref[32 * z + 16 : 32 * z + 32] = grad[1, row] * flag
    keep[256:264] = jnp.broadcast_to(misfit, (8, NZ))
    send[256:264] = jnp.broadcast_to(misfit, (8, NZ))


def pair_kernel(mine, other, out):
    misfit = mine[256:264] + other[256:264]
    for z in range(8):
        out[z, 0:32] = mine[32 * z : 32 * z + 32] + other[32 * z : 32 * z + 32]
        out[z, 32:40] = misfit


def sum_kernel(blocks, part, misfit):
    total = blocks[0]
    for z in range(1, 8):
        total = total + blocks[z]
    part[0, 0, 0, 0] = total[0:16]
    part[0, 0, 1, 0] = total[16:32]
    misfit[...] = total[32:33, 0:1]


def on_device(cond_h, cond_v, fwd_init, adj_init, observed, footprint, owner, rec_cells):
    halos = exchange(*pack(fwd_init, cond_h, cond_v, adj_init))
    rec = rec_cells.reshape(32)
    coef, stored, spread, block = pl.pallas_call(
        forward_kernel,
        out_shape=[
            shape(4, EXP, EY, NZ),
            shape(STEPS, 3, CX, CY, NZ),
            shape(CY, NZ),
            shape(16, 16, NZ),
        ],
        in_specs=[VMEM] * 10 + [SMEM],
        out_specs=[VMEM] * 4,
        scratch_shapes=[
            pltpu.VMEM((3, EXP, EY, NZ), F32),
            pltpu.VMEM((3, EXP, EY, NZ), F32),
            pltpu.VMEM((256, NZ), F32),
        ],
        compiler_params=params(),
        name="forward",
    )(fwd_init, cond_h, cond_v, *halos, observed.reshape(8, 32), rec.reshape(1, 32), rec)
    blocks = lax.all_to_all(block, ("gx", "gy"), 0, 0, tiled=True)
    keep, send = pl.pallas_call(
        adjoint_kernel,
        out_shape=[shape(264, NZ)] * 2,
        in_specs=[VMEM] * 10 + [SMEM, SMEM],
        out_specs=[VMEM] * 2,
        scratch_shapes=[
            pltpu.VMEM((3, EXP, EY, NZ), F32),
            pltpu.VMEM((3, EXP, EY, NZ), F32),
            pltpu.VMEM((3, EY, NZ), F32),
            pltpu.VMEM((2, CX, CY, NZ), F32),
        ],
        compiler_params=params(),
        name="adjoint",
    )(
        adj_init,
        *halos,
        coef,
        stored,
        spread,
        blocks,
        footprint.reshape(1),
        owner.reshape(16),
    )
    size = lax.axis_size("tx")
    other = lax.ppermute(send, "tx", [(t, t ^ 1) for t in range(size)])
    paired = pl.pallas_call(
        pair_kernel,
        out_shape=shape(8, 40, NZ),
        in_specs=[VMEM] * 2,
        out_specs=VMEM,
        compiler_params=params(),
        name="pair",
    )(keep, other)
    along_z = [list(range(core, size, 2)) for core in range(2)]
    summed = lax.all_to_all(paired, "tx", 0, 0, axis_index_groups=along_z, tiled=True)
    part, misfit = pl.pallas_call(
        sum_kernel,
        out_shape=[shape(1, 1, 2, 1, CY, NZ), shape(1, 1)],
        in_specs=[VMEM],
        out_specs=[VMEM, VMEM],
        compiler_params=params(),
        name="total",
    )(summed)
    return part, misfit.reshape(())


def solution(mesh):
    placed = (
        P("gx", "gy", None),
        P("gx", "gy", None),
        P("tx", None, "gx", "gy", None),
        P("tx", None, "gx", "gy", None),
        P("tx", None, "gx", "gy", None, None),
        P("tx", "gx", "gy"),
        P("gx", "gy", None),
        P("gx", "gy", None),
    )
    return jax.shard_map(
        on_device,
        mesh=mesh,
        in_specs=placed,
        out_specs=(P("gx", "tx", None, None, "gy", None), P()),
        check_vma=False,
    )
```

```python
import jax
import jax.numpy as jnp
from jax import lax
from jax.experimental import pallas as pl
from jax.experimental.pallas import tpu as pltpu
from jax.sharding import PartitionSpec as P

STEPS = 4
ZREC = 32
STEP_DT = 0.5
HALO = 4
CX = 16
CY = 16
NZ = 128
EX = CX + 2 * HALO
EXP = EX + 4
EY = CY + 2 * HALO
F32 = jnp.float32
HIGHEST = lax.Precision.HIGHEST

LOW = [(c, x) for c in range(8) for x in range(CX - HALO + (c in (3, 6, 7)), CX)]
HIGH = [(c, x) for c in range(8) for x in range(HALO - (c not in (1, 2)))]
ADJ_LOW = [(c, x) for c, x in LOW if c < 6]
ADJ_HIGH = [(c, x) for c, x in HIGH if c < 6]
VMEM = pl.BlockSpec(memory_space=pltpu.VMEM)
SMEM = pl.BlockSpec(memory_space=pltpu.SMEM)
HBM = pl.BlockSpec(memory_space=pltpu.HBM)


def shape(*dims):
    return jax.ShapeDtypeStruct(dims, F32)


def in_hbm(array):
    return pltpu.with_memory_space_constraint(array, pltpu.HBM)


def params():
    return pltpu.CompilerParams(vmem_limit_bytes=8 * 1024 * 1024)


def plane_of(refs, comp, x):
    return refs[0][0, comp, x] if comp < 6 else refs[comp - 5][x]


def edge_of(plane, second):
    return jnp.where(second, plane[0:HALO], plane[CY - HALO : CY])


def pack_kernel(fwd, cond_h, cond_v, adj, *refs):
    to_next, to_prev, to_side, side_next, side_prev, adj_next, adj_prev = refs[:7]
    bufs, sem = refs[7:11], refs[11]
    copies = [
        pltpu.make_async_copy(src, dst, sem.at[k])
        for k, (src, dst) in enumerate(zip((fwd, cond_h, cond_v, adj), bufs))
    ]
    for copy in copies:
        copy.start()
    second = lax.axis_index("gy") == 1
    for which, comps in ((0, range(6)), (1, (6,)), (2, (7,))):
        copies[which].wait()
        for c in comps:
            edges = [edge_of(plane_of(bufs, c, x), second) for x in range(CX)]
            for x in range(CX):
                to_side[c, x] = edges[x]
            for k, (comp, x) in enumerate(LOW):
                if comp == c:
                    to_next[k] = plane_of(bufs, c, x)
                    side_next[k] = edges[x]
            for k, (comp, x) in enumerate(HIGH):
                if comp == c:
                    to_prev[k] = plane_of(bufs, c, x)
                    side_prev[k] = edges[x]
    copies[3].wait()
    for k, (c, x) in enumerate(ADJ_LOW):
        adj_next[k] = bufs[3][0, c, x]
    for k, (c, x) in enumerate(ADJ_HIGH):
        adj_prev[k] = bufs[3][0, c, x]


def pack(*arrays):
    return pl.pallas_call(
        pack_kernel,
        out_shape=[
            shape(len(LOW), CY, NZ),
            shape(len(HIGH), CY, NZ),
            shape(8, CX, HALO, NZ),
            shape(len(LOW), HALO, NZ),
            shape(len(HIGH), HALO, NZ),
            shape(len(ADJ_LOW), CY, NZ),
            shape(len(ADJ_HIGH), CY, NZ),
        ],
        in_specs=[HBM] * 4,
        out_specs=[VMEM] * 7,
        scratch_shapes=[pltpu.VMEM(a.shape, F32) for a in arrays]
        + [pltpu.SemaphoreType.DMA((4,))],
        compiler_params=params(),
        name="pack",
    )(*(in_hbm(a) for a in arrays))


def pack_side_kernel(adj, from_prev, from_next, to_side):
    second = lax.axis_index("gy") == 1
    for c in range(6):
        for x in range(CX):
            to_side[c, HALO + x] = edge_of(adj[0, c, x], second)
        filled = set(range(HALO, HALO + CX))
        for k, (comp, x) in enumerate(ADJ_LOW):
            if comp == c:
                to_side[c, x - (CX - HALO)] = edge_of(from_prev[k], second)
                filled.add(x - (CX - HALO))
        for k, (comp, x) in enumerate(ADJ_HIGH):
            if comp == c:
                to_side[c, x + HALO + CX] = edge_of(from_next[k], second)
                filled.add(x + HALO + CX)
        for i in range(EX):
            if i not in filled:
                to_side[c, i] = jnp.zeros((HALO, NZ), F32)


def pairs(dx, swap):
    size_x = lax.axis_size("gx")
    size_y = lax.axis_size("gy")
    return [
        (x * size_y + y, (x + dx) * size_y + (1 - y if swap else y))
        for x in range(size_x)
        for y in range(size_y)
        if 0 <= x + dx < size_x
    ]


def send(array, dx, swap):
    return lax.ppermute(array, ("gx", "gy"), pairs(dx, swap))


def assemble(own, halos, comps, first):
    from_prev, from_next, from_side, side_prev, side_next = halos
    zero_rows = jnp.zeros((HALO, NZ), F32)
    zero_plane = jnp.zeros((EY, NZ), F32)

    def put(ref, index, i, plane, rows):
        ref[index, i, 0:CY] = plane
        ref[index, i, CY : CY + HALO] = jnp.where(first, rows, zero_rows)
        ref[index, i, CY + HALO : EY] = jnp.where(first, zero_rows, rows)

    for c, (ref, index) in comps.items():
        filled = set()
        for x in range(CX):
            put(ref, index, HALO + x, own(c, x), from_side[c, x])
            filled.add(HALO + x)
        for k, (comp, x) in enumerate(LOW):
            if comp == c:
                i = x - (CX - HALO)
                put(ref, index, i, from_prev[k], side_prev[k])
                filled.add(i)
        for k, (comp, x) in enumerate(HIGH):
            if comp == c:
                i = x + HALO + CX
                put(ref, index, i, from_next[k], side_next[k])
                filled.add(i)
        for i in range(EXP):
            if i not in filled:
                ref[index, i] = zero_plane


def helpers(gy):
    lane = lax.broadcasted_iota(jnp.int32, (EY, NZ), 1)
    row = lax.broadcasted_iota(jnp.int32, (EY, NZ), 0)
    y = jnp.where(row < CY + HALO, row, row - EY) + gy * CY
    inside = (y >= 0) & (y < 2 * CY)
    last, start = lane == NZ - 1, lane == 0

    def z_up(f):
        return jnp.where(last, 0.0, pltpu.roll(f, NZ - 1, 1))

    def z_down(f):
        return jnp.where(start, 0.0, pltpu.roll(f, 1, 1))

    def y_up(f):
        return pltpu.roll(f, EY - 1, 0)

    def y_down(f):
        return pltpu.roll(f, 1, 0)

    return lane, inside, z_up, z_down, y_up, y_down


def in_grid(gx, i):
    x = gx * CX + i - HALO
    return (x >= 0) & (x < 8 * CX)


MODE = "fused"
UNROLL = 8


def sweep(step, gx, elec, mag, coef, tools):
    _, inside, z_up, z_down, y_up, y_down = tools
    half = jnp.where(inside, STEP_DT, 0.0)
    zero = jnp.zeros((EY, NZ), F32)
    turns = -(-(EX - 1 - 2 * step) // UNROLL)

    def magnetic(i, field, after):
        ex, ey, ez = field
        _, ey_next, ez_next = after
        rate = jnp.where(in_grid(gx, i), half, zero)
        hx = mag[0, i] - rate * ((y_up(ez) - ez) - (z_up(ey) - ey))
        hy = mag[1, i] - rate * ((z_up(ex) - ex) - (ez_next - ez))
        hz = mag[2, i] - rate * ((ey_next - ey) - (y_up(ex) - ex))
        return hx, hy, hz

    def electric(i, field, now, before):
        ex, ey, ez = field
        hx, hy, hz = now
        decay_h, drive_h, decay_v, drive_v = (coef[k, i] for k in range(4))
        ex = decay_h * ex + drive_h * ((hz - y_down(hz)) - (hy - z_down(hy)))
        ey = decay_h * ey + drive_h * ((hx - z_down(hx)) - (hz - before[2]))
        ez = decay_v * ez + drive_v * ((hy - before[1]) - (hx - y_down(hx)))
        return ex, ey, ez

    def planes(ref, i, n):
        return [tuple(ref[c, i + k] for c in range(3)) for k in range(n)]

    def put(ref, i, values):
        for k, plane in enumerate(values):
            for c in range(3):
                ref[c, i + k] = plane[c]

    if MODE == "fused":

        def body(turn, carry):
            i = step + turn * UNROLL
            field = planes(elec, i, UNROLL + 1)
            now = [magnetic(i + k, field[k], field[k + 1]) for k in range(UNROLL)]
            put(mag, i, now)
            before = [(None, *carry)] + now[:-1]
            put(elec, i, [electric(i + k, field[k], now[k], before[k]) for k in range(UNROLL)])
            return now[-1][1:]

        lax.fori_loop(0, turns, body, (zero, zero))
    else:

        def body_h(turn, carry):
            i = step + turn * UNROLL
            field = planes(elec, i, UNROLL + 1)
            put(mag, i, [magnetic(i + k, field[k], field[k + 1]) for k in range(UNROLL)])
            return carry

        def body_e(turn, carry):
            i = step + 1 + turn * UNROLL
            field = planes(elec, i, UNROLL)
            now = planes(mag, i - 1, UNROLL + 1)
            put(elec, i, [electric(i + k, field[k], now[k + 1], now[k]) for k in range(UNROLL)])
            return carry

        lax.fori_loop(0, turns, body_h, 0)
        lax.fori_loop(0, -(-(EX - 2 - 2 * step) // UNROLL), body_e, 0)


def forward_kernel(fwd, cond_h, cond_v, *refs):
    halos, refs = refs[:5], refs[5:]
    observed, rec_vec, rec, coef_out, stored_out, spread, block = refs[:7]
    coef, stored, elec, mag, rows, sem = refs[7:]
    gx, gy = lax.axis_index("gx"), lax.axis_index("gy")
    tools = helpers(gy)
    lane, inside = tools[0], tools[1]

    comps = {c: (elec, c) if c < 3 else (mag, c - 3) for c in range(6)}
    comps |= {6: (coef, 0), 7: (coef, 2)}
    assemble(lambda c, x: plane_of((fwd, cond_h, cond_v, None), c, x), halos, comps, gy == 0)

    def coefficients(i, carry):
        keep = inside & in_grid(gx, i)
        for k in (0, 2):
            half_rate = 0.25 * coef[k, i]
            inverse = 1.0 / (1.0 + half_rate)
            coef[k, i] = jnp.where(keep, (1.0 - half_rate) * inverse, 0.0)
            coef[k + 1, i] = jnp.where(keep, STEP_DT * inverse, 0.0)
        return carry

    lax.fori_loop(0, EX, coefficients, 0)
    for k in (1, 3):
        coef[k, EX:EXP] = jnp.zeros((EXP - EX, EY, NZ), F32)

    copies = [pltpu.make_async_copy(coef, coef_out, sem.at[STEPS])]
    copies[0].start()
    for step in range(STEPS):
        sweep(step, gx, elec, mag, coef, tools)
        stored[step] = elec[:, HALO : HALO + CX, 0:CY]
        copies.append(pltpu.make_async_copy(stored.at[step], stored_out.at[step], sem.at[step]))
        copies[-1].start()

    for r in range(rec.shape[0]):
        x, y = rec[r] >> 4, rec[r] & 15
        for step in range(STEPS):
            for c in range(2):
                rows[pl.ds((2 * step + c) * 32 + r, 1), :] = stored[step, c, x, pl.ds(y, 1), :]
    pick = (lax.broadcasted_iota(jnp.int32, (8, NZ), 1) == ZREC).astype(F32)
    picked = lax.dot_general(
        pick, rows[...], (((1,), (1,)), ((), ())), precision=HIGHEST, preferred_element_type=F32
    )
    lane8 = lax.broadcasted_iota(jnp.int32, (8, NZ), 1)
    row8 = lax.broadcasted_iota(jnp.int32, (8, NZ), 0)
    own = jnp.where(lane8 // 32 == row8, picked[:, 0:NZ], 0.0)
    own = own + jnp.where(lane8 // 32 + 4 == row8, picked[:, NZ : 2 * NZ], 0.0)
    own = own + pltpu.roll(own, 64, 1)
    own = own + pltpu.roll(own, 32, 1)
    residual = own[:, 0:32] - observed[...]
    misfit = 0.5 * jnp.sum(residual * residual)
    cells = rec_vec[...]
    at_y = ((cells & 15) == lax.broadcasted_iota(jnp.int32, (CY, 32), 0)).astype(F32)
    at_x = (cells >> 4) == lax.broadcasted_iota(jnp.int32, (NZ, 32), 0) // 8
    weighted = jnp.where(at_x, jnp.tile(residual, (16, 1)), 0.0)
    spread_now = lax.dot_general(
        at_y, weighted, (((1,), (1,)), ((), ())), precision=HIGHEST, preferred_element_type=F32
    )
    spread[...] = spread_now
    low_rows, high_rows = spread_now[0:8], spread_now[8:16]
    edges = jnp.where((lane8 < 32) | (lane8 >= 96), low_rows, pltpu.roll(high_rows, 64, 1))
    is_first = gy == 0
    side = jnp.where(is_first, high_rows, low_rows)
    used = row8 // HALO == 1 - gy
    side = jnp.where(used, side, misfit)
    for t in range(16):
        block[t, 0:8] = edges
        block[t, 8:16] = side
    for copy in copies:
        copy.wait()


def adjoint_kernel(adj, from_prev, from_next, from_side, coef_in, stored_in, *refs):
    spread, blocks, foot, owner, keep, away = refs[:6]
    coef, stored, elec, mag, inject, grad, sem = refs[6:]
    gx, gy = lax.axis_index("gx"), lax.axis_index("gy")
    tools = helpers(gy)
    lane, inside = tools[0], tools[1]

    copies = [
        pltpu.make_async_copy(adj.at[0, 0:3], elec.at[:, HALO : HALO + CX, 0:CY], sem.at[0]),
        pltpu.make_async_copy(adj.at[0, 3:6], mag.at[:, HALO : HALO + CX, 0:CY], sem.at[1]),
        pltpu.make_async_copy(coef_in, coef, sem.at[2]),
        pltpu.make_async_copy(stored_in, stored, sem.at[3]),
    ]
    for copy in copies:
        copy.start()
    zero_rows = jnp.zeros((HALO, NZ), F32)
    zero_plane = jnp.zeros((EY, NZ), F32)
    targets = [(elec, c) for c in range(3)] + [(mag, c) for c in range(3)]
    for c, (ref, index) in enumerate(targets):
        filled = set(range(HALO, HALO + CX))
        for source, planes, base in (
            (from_prev, ADJ_LOW, HALO - CX),
            (from_next, ADJ_HIGH, HALO + CX),
        ):
            for k, (comp, x) in enumerate(planes):
                if comp == c:
                    ref[index, x + base, 0:CY] = source[k]
                    filled.add(x + base)
        for i in range(EXP):
            if i not in filled:
                ref[index, i] = zero_plane

    row8 = lax.broadcasted_iota(jnp.int32, (8, NZ), 0)
    used = row8 // HALO == gy
    for k, dx in enumerate((-1, 0, 1)):
        there = (gx + dx >= 0) & (gx + dx < 8)
        near = jnp.clip(gx + dx, 0, 7)
        if dx == 0:
            inject[k, 0:16] = spread[...]
        else:
            edges = jnp.where(there, blocks[2 * near + gy, 0:8], 0.0)
            inject[k, 0:8] = edges
            inject[k, 8:16] = pltpu.roll(edges, 64, 1)
        side = blocks[2 * near + 1 - gy, 8:16]
        inject[k, 16:24] = jnp.where(used & there, side, 0.0)

    first = gy == 0
    for c, (ref, index) in enumerate(targets):
        for i in range(EX):
            rows = from_side[c, i]
            ref[index, i, CY : CY + HALO] = jnp.where(first, rows, zero_rows)
            ref[index, i, CY + HALO : EY] = jnp.where(first, zero_rows, rows)
    for copy in copies:
        copy.wait()

    at_depth = lane == ZREC

    for step in range(STEPS):
        when = STEPS - 1 - step

        def add(turn, carry, when=when):
            for k in range(4):
                i = turn * 4 + k
                tile = jnp.where(turn == 0, 0, jnp.where(turn < 5, 1, 2))
                x = (i + CX - HALO) & (CX - 1)
                source = inject[tile]
                shift = (ZREC + NZ - (x * 8 + 2 * when)) & (NZ - 1)
                for c in range(2):
                    moved = pltpu.roll(source, (shift - c) & (NZ - 1), 1)
                    elec[c, i] += jnp.where(at_depth, moved, 0.0)
            return carry

        lax.fori_loop(0, EX // 4, add, 0)
        sweep(step, gx, elec, mag, coef, tools)

        def accumulate(x, carry, when=when, step=step):
            ax, ay, az = (elec[c, HALO + x, 0:CY] for c in range(3))
            horizontal = ax * stored[when, 0, x] + ay * stored[when, 1, x]
            vertical = az * stored[when, 2, x]
            if step:
                horizontal = grad[0, x] + horizontal
                vertical = grad[1, x] + vertical
            grad[0, x] = horizontal
            grad[1, x] = vertical
            return carry

        lax.fori_loop(0, CX, accumulate, 0)

    flag = foot[0].astype(F32)
    misfit = blocks[0, 8:16][0:1]
    for t in range(1, 16):
        top = 0 if t % 2 == 0 else HALO
        misfit = misfit + blocks[t, 8:16][top : top + 1]
    core = lax.axis_index("tx") & 1
    for z in range(8):
        for ref, mine in ((keep, core), (away, 1 - core)):
            row = owner[2 * z + mine]
            ref[32 * z : 32 * z + 16] = grad[0, row] * flag
            ref[32 * z + 16 : 32 * z + 32] = grad[1, row] * flag
    keep[256:264] = jnp.broadcast_to(misfit, (8, NZ))
    away[256:264] = jnp.broadcast_to(misfit, (8, NZ))


def pair_kernel(mine, other, out):
    misfit = mine[256:264] + other[256:264]
    for z in range(8):
        out[z, 0:32] = mine[32 * z : 32 * z + 32] + other[32 * z : 32 * z + 32]
        out[z, 32:40] = misfit


def sum_kernel(blocks, part, misfit):
    total = blocks[0]
    for z in range(1, 8):
        total = total + blocks[z]
    part[0, 0, 0, 0] = total[0:16]
    part[0, 0, 1, 0] = total[16:32]
    misfit[...] = total[32:33, 0:1]


def on_device(cond_h, cond_v, fwd_init, adj_init, observed, footprint, owner, rec_cells):
    packed = pack(fwd_init, cond_h, cond_v, adj_init)
    to_next, to_prev, to_side, side_next, side_prev, adj_next, adj_prev = packed
    halos = (
        send(to_next, 1, False),
        send(to_prev, -1, False),
        send(to_side, 0, True),
        send(side_next, 1, True),
        send(side_prev, -1, True),
    )
    adj_halos = (send(adj_next, 1, False), send(adj_prev, -1, False))
    rec = rec_cells.reshape(32)
    coef, stored, spread, block = pl.pallas_call(
        forward_kernel,
        out_shape=[
            pltpu.HBM((4, EXP, EY, NZ), F32),
            pltpu.HBM((STEPS, 3, CX, CY, NZ), F32),
            shape(CY, NZ),
            shape(16, 16, NZ),
        ],
        in_specs=[VMEM] * 10 + [SMEM],
        out_specs=[HBM, HBM, VMEM, VMEM],
        scratch_shapes=[
            pltpu.VMEM((4, EXP, EY, NZ), F32),
            pltpu.VMEM((STEPS, 3, CX, CY, NZ), F32),
            pltpu.VMEM((3, EXP, EY, NZ), F32),
            pltpu.VMEM((3, EXP, EY, NZ), F32),
            pltpu.VMEM((256, NZ), F32),
            pltpu.SemaphoreType.DMA((STEPS + 1,)),
        ],
        compiler_params=params(),
        name="forward",
    )(fwd_init, cond_h, cond_v, *halos, observed.reshape(8, 32), rec.reshape(1, 32), rec)
    block, *adj_ready = lax.optimization_barrier((block, *adj_halos))
    adj_side = pl.pallas_call(
        pack_side_kernel,
        out_shape=shape(6, EX, HALO, NZ),
        in_specs=[VMEM] * 3,
        out_specs=VMEM,
        compiler_params=params(),
        name="pack_side",
    )(adj_init, *adj_ready)
    block, adj_side = lax.optimization_barrier((block, adj_side))
    from_side = send(adj_side, 0, True)
    blocks = lax.all_to_all(block, ("gx", "gy"), 0, 0, tiled=True)
    keep, away = pl.pallas_call(
        adjoint_kernel,
        out_shape=[shape(264, NZ)] * 2,
        in_specs=[HBM] + [VMEM] * 3 + [HBM] * 2 + [VMEM] * 2 + [SMEM, SMEM],
        out_specs=[VMEM] * 2,
        scratch_shapes=[
            pltpu.VMEM((4, EXP, EY, NZ), F32),
            pltpu.VMEM((STEPS, 3, CX, CY, NZ), F32),
            pltpu.VMEM((3, EXP, EY, NZ), F32),
            pltpu.VMEM((3, EXP, EY, NZ), F32),
            pltpu.VMEM((3, EY, NZ), F32),
            pltpu.VMEM((2, CX, CY, NZ), F32),
            pltpu.SemaphoreType.DMA((4,)),
        ],
        compiler_params=params(),
        name="adjoint",
    )(
        in_hbm(adj_init),
        *adj_halos,
        from_side,
        in_hbm(coef),
        in_hbm(stored),
        spread,
        blocks,
        footprint.reshape(1),
        owner.reshape(16),
    )
    size = lax.axis_size("tx")
    other = lax.ppermute(away, "tx", [(t, t ^ 1) for t in range(size)])
    paired = pl.pallas_call(
        pair_kernel,
        out_shape=shape(8, 40, NZ),
        in_specs=[VMEM] * 2,
        out_specs=VMEM,
        compiler_params=params(),
        name="pair",
    )(keep, other)
    along_z = [list(range(core, size, 2)) for core in range(2)]
    summed = lax.all_to_all(paired, "tx", 0, 0, axis_index_groups=along_z, tiled=True)
    part, misfit = pl.pallas_call(
        sum_kernel,
        out_shape=[shape(1, 1, 2, 1, CY, NZ), shape(1, 1)],
        in_specs=[VMEM],
        out_specs=[VMEM, VMEM],
        compiler_params=params(),
        name="total",
    )(summed)
    return part, misfit.reshape(())


def solution(mesh):
    placed = (
        P("gx", "gy", None),
        P("gx", "gy", None),
        P("tx", None, "gx", "gy", None),
        P("tx", None, "gx", "gy", None),
        P("tx", None, "gx", "gy", None, None),
        P("tx", "gx", "gy"),
        P("gx", "gy", None),
        P("gx", "gy", None),
    )
    return jax.shard_map(
        on_device,
        mesh=mesh,
        in_specs=placed,
        out_specs=(P("gx", "tx", None, None, "gy", None), P()),
        check_vma=False,
    )
```

```python
import jax
import jax.numpy as jnp
from jax import lax
from jax.experimental import pallas as pl
from jax.experimental.pallas import tpu as pltpu
from jax.sharding import PartitionSpec as P

STEPS = 4
ZREC = 32
STEP_DT = 0.5
HALO = 4
CX = 16
CY = 16
NZ = 128
EX = CX + 2 * HALO
EXP = EX + 4
EY = CY + 2 * HALO
F32 = jnp.float32
HIGHEST = lax.Precision.HIGHEST

LOW = [(c, x) for c in range(8) for x in range(CX - HALO + (c in (3, 6, 7)), CX)]
HIGH = [(c, x) for c in range(8) for x in range(HALO - (c not in (1, 2)))]
ADJ_LOW = [(c, x) for c, x in LOW if c < 6]
ADJ_HIGH = [(c, x) for c, x in HIGH if c < 6]
VMEM = pl.BlockSpec(memory_space=pltpu.VMEM)
SMEM = pl.BlockSpec(memory_space=pltpu.SMEM)
HBM = pl.BlockSpec(memory_space=pltpu.HBM)


def shape(*dims):
    return jax.ShapeDtypeStruct(dims, F32)


def in_hbm(array):
    return pltpu.with_memory_space_constraint(array, pltpu.HBM)


def params():
    return pltpu.CompilerParams(vmem_limit_bytes=8 * 1024 * 1024)


def plane_of(refs, comp, x):
    return refs[0][0, comp, x] if comp < 6 else refs[comp - 5][x]


def edge_of(plane, second):
    return jnp.where(second, plane[0:HALO], plane[CY - HALO : CY])


def pack_kernel(fwd, cond_h, cond_v, adj, *refs):
    to_next, to_prev, to_side, side_next, side_prev, adj_next, adj_prev = refs[:7]
    bufs, sem = refs[7:11], refs[11]
    copies = [
        pltpu.make_async_copy(src, dst, sem.at[k])
        for k, (src, dst) in enumerate(zip((fwd, cond_h, cond_v, adj), bufs))
    ]
    for copy in copies:
        copy.start()
    second = lax.axis_index("gy") == 1
    for which, comps in ((0, range(6)), (1, (6,)), (2, (7,))):
        copies[which].wait()
        for c in comps:
            edges = [edge_of(plane_of(bufs, c, x), second) for x in range(CX)]
            for x in range(CX):
                to_side[c, x] = edges[x]
            for k, (comp, x) in enumerate(LOW):
                if comp == c:
                    to_next[k] = plane_of(bufs, c, x)
                    side_next[k] = edges[x]
            for k, (comp, x) in enumerate(HIGH):
                if comp == c:
                    to_prev[k] = plane_of(bufs, c, x)
                    side_prev[k] = edges[x]
    copies[3].wait()
    for k, (c, x) in enumerate(ADJ_LOW):
        adj_next[k] = bufs[3][0, c, x]
    for k, (c, x) in enumerate(ADJ_HIGH):
        adj_prev[k] = bufs[3][0, c, x]


def pack(*arrays):
    return pl.pallas_call(
        pack_kernel,
        out_shape=[
            shape(len(LOW), CY, NZ),
            shape(len(HIGH), CY, NZ),
            shape(8, CX, HALO, NZ),
            shape(len(LOW), HALO, NZ),
            shape(len(HIGH), HALO, NZ),
            shape(len(ADJ_LOW), CY, NZ),
            shape(len(ADJ_HIGH), CY, NZ),
        ],
        in_specs=[HBM] * 4,
        out_specs=[VMEM] * 7,
        scratch_shapes=[pltpu.VMEM(a.shape, F32) for a in arrays]
        + [pltpu.SemaphoreType.DMA((4,))],
        compiler_params=params(),
        name="pack",
    )(*(in_hbm(a) for a in arrays))


def pack_side_kernel(adj, from_prev, from_next, to_side):
    second = lax.axis_index("gy") == 1
    for c in range(6):
        for x in range(CX):
            to_side[c, HALO + x] = edge_of(adj[0, c, x], second)
        filled = set(range(HALO, HALO + CX))
        for k, (comp, x) in enumerate(ADJ_LOW):
            if comp == c:
                to_side[c, x - (CX - HALO)] = edge_of(from_prev[k], second)
                filled.add(x - (CX - HALO))
        for k, (comp, x) in enumerate(ADJ_HIGH):
            if comp == c:
                to_side[c, x + HALO + CX] = edge_of(from_next[k], second)
                filled.add(x + HALO + CX)
        for i in range(EX):
            if i not in filled:
                to_side[c, i] = jnp.zeros((HALO, NZ), F32)


def pairs(dx, swap):
    size_x = lax.axis_size("gx")
    size_y = lax.axis_size("gy")
    return [
        (x * size_y + y, (x + dx) * size_y + (1 - y if swap else y))
        for x in range(size_x)
        for y in range(size_y)
        if 0 <= x + dx < size_x
    ]


def send(array, dx, swap):
    return lax.ppermute(array, ("gx", "gy"), pairs(dx, swap))


def assemble(own, halos, comps, first):
    from_prev, from_next, from_side, side_prev, side_next = halos
    zero_rows = jnp.zeros((HALO, NZ), F32)
    zero_plane = jnp.zeros((EY, NZ), F32)

    def put(ref, index, i, plane, rows):
        ref[index, i, 0:CY] = plane
        ref[index, i, CY : CY + HALO] = jnp.where(first, rows, zero_rows)
        ref[index, i, CY + HALO : EY] = jnp.where(first, zero_rows, rows)

    for c, (ref, index) in comps.items():
        filled = set()
        for x in range(CX):
            put(ref, index, HALO + x, own(c, x), from_side[c, x])
            filled.add(HALO + x)
        for k, (comp, x) in enumerate(LOW):
            if comp == c:
                i = x - (CX - HALO)
                put(ref, index, i, from_prev[k], side_prev[k])
                filled.add(i)
        for k, (comp, x) in enumerate(HIGH):
            if comp == c:
                i = x + HALO + CX
                put(ref, index, i, from_next[k], side_next[k])
                filled.add(i)
        for i in range(EXP):
            if i not in filled:
                ref[index, i] = zero_plane


def helpers(gy):
    lane = lax.broadcasted_iota(jnp.int32, (EY, NZ), 1)
    row = lax.broadcasted_iota(jnp.int32, (EY, NZ), 0)
    y = jnp.where(row < CY + HALO, row, row - EY) + gy * CY
    inside = (y >= 0) & (y < 2 * CY)
    last, start = lane == NZ - 1, lane == 0

    def z_up(f):
        return jnp.where(last, 0.0, pltpu.roll(f, NZ - 1, 1))

    def z_down(f):
        return jnp.where(start, 0.0, pltpu.roll(f, 1, 1))

    def y_up(f):
        return pltpu.roll(f, EY - 1, 0)

    def y_down(f):
        return pltpu.roll(f, 1, 0)

    return lane, inside, z_up, z_down, y_up, y_down


def in_grid(gx, i):
    x = gx * CX + i - HALO
    return (x >= 0) & (x < 8 * CX)


UNROLL = 24


def sweep(step, gx, elec, mag, coef, tools):
    _, inside, z_up, z_down, y_up, y_down = tools
    half = jnp.where(inside, STEP_DT, 0.0)
    zero = jnp.zeros((EY, NZ), F32)
    count = EX - 1 - 2 * step
    unroll = min(UNROLL, count)
    turns = -(-count // unroll)

    def magnetic(i, field, after):
        ex, ey, ez = field
        _, ey_next, ez_next = after
        rate = jnp.where(in_grid(gx, i), half, zero)
        hx = mag[0, i] - rate * ((y_up(ez) - ez) - (z_up(ey) - ey))
        hy = mag[1, i] - rate * ((z_up(ex) - ex) - (ez_next - ez))
        hz = mag[2, i] - rate * ((ey_next - ey) - (y_up(ex) - ex))
        return hx, hy, hz

    def electric(i, field, now, before):
        ex, ey, ez = field
        hx, hy, hz = now
        decay_h, drive_h, decay_v, drive_v = (coef[k, i] for k in range(4))
        ex = decay_h * ex + drive_h * ((hz - y_down(hz)) - (hy - z_down(hy)))
        ey = decay_h * ey + drive_h * ((hx - z_down(hx)) - (hz - before[2]))
        ez = decay_v * ez + drive_v * ((hy - before[1]) - (hx - y_down(hx)))
        return ex, ey, ez

    def planes(ref, i, n):
        return [tuple(ref[c, i + k] for c in range(3)) for k in range(n)]

    def put(ref, i, values):
        for k, plane in enumerate(values):
            for c in range(3):
                ref[c, i + k] = plane[c]

    def body(turn, carry):
        i = step + turn * unroll
        field = planes(elec, i, unroll + 1)
        now = [magnetic(i + k, field[k], field[k + 1]) for k in range(unroll)]
        put(mag, i, now)
        before = [(None, *carry)] + now[:-1]
        put(elec, i, [electric(i + k, field[k], now[k], before[k]) for k in range(unroll)])
        return now[-1][1:]

    if turns == 1:
        body(0, (zero, zero))
    else:
        lax.fori_loop(0, turns, body, (zero, zero))


def dot(a, b, dim_a, dim_b):
    dims = (((dim_a,), (dim_b,)), ((), ()))
    return lax.dot_general(a, b, dims, precision=HIGHEST, preferred_element_type=F32)


def forward_kernel(fwd, cond_h, cond_v, *refs):
    halos, refs = refs[:5], refs[5:]
    observed, rec_vec, coef_out, stored_out, spread, block = refs[:6]
    coef, stored, elec, mag, sem = refs[6:]
    gx, gy = lax.axis_index("gx"), lax.axis_index("gy")
    tools = helpers(gy)
    lane, inside = tools[0], tools[1]

    comps = {c: (elec, c) if c < 3 else (mag, c - 3) for c in range(6)}
    comps |= {6: (coef, 0), 7: (coef, 2)}
    assemble(lambda c, x: plane_of((fwd, cond_h, cond_v, None), c, x), halos, comps, gy == 0)

    def coefficients(turn, carry):
        for i in [turn * 8 + k for k in range(8)]:
            keep = inside & in_grid(gx, i)
            for k in (0, 2):
                half_rate = 0.25 * coef[k, i]
                inverse = 1.0 / (1.0 + half_rate)
                coef[k, i] = jnp.where(keep, (1.0 - half_rate) * inverse, 0.0)
                coef[k + 1, i] = jnp.where(keep, STEP_DT * inverse, 0.0)
        return carry

    lax.fori_loop(0, EX // 8, coefficients, 0)
    for k in (1, 3):
        coef[k, EX:EXP] = jnp.zeros((EXP - EX, EY, NZ), F32)

    cells = rec_vec[...]
    at_y = ((cells & 15) == lax.broadcasted_iota(jnp.int32, (CY, 32), 0)).astype(F32)
    cell_x = ((cells >> 4) == lax.broadcasted_iota(jnp.int32, (CX, 32), 0)).astype(F32)
    lane_x = lax.broadcasted_iota(jnp.int32, (CX, NZ), 1) >> 3
    lane_q = lax.broadcasted_iota(jnp.int32, (8, NZ), 1) & 7
    at_x = dot(cell_x, (lane_x == lax.broadcasted_iota(jnp.int32, (CX, NZ), 0)).astype(F32), 0, 0)
    target = dot(
        observed[...], (lane_q == lax.broadcasted_iota(jnp.int32, (8, NZ), 0)).astype(F32), 0, 0
    )
    copies = [pltpu.make_async_copy(coef, coef_out, sem.at[STEPS])]
    copies[0].start()
    for step in range(STEPS):
        sweep(step, gx, elec, mag, coef, tools)
        stored[step] = elec[:, HALO : HALO + CX, 0:CY]
        copies.append(pltpu.make_async_copy(stored.at[step], stored_out.at[step], sem.at[step]))
        copies[-1].start()

    at_depth = lane[0:CY] == ZREC
    record = jnp.zeros((CY, NZ), F32)
    for x in range(CX):
        for q in range(8):
            column = jnp.where(at_depth, stored[q // 2, q % 2, x], 0.0)
            record = record + pltpu.roll(column, (x * 8 + q - ZREC) % NZ, 1)
    at_receivers = dot(at_y, record, 0, 0)
    residual = at_x * (at_receivers - target)
    misfit = 0.5 * jnp.sum(residual * residual)
    spread_now = dot(at_y, residual, 1, 0)
    lane8 = lax.broadcasted_iota(jnp.int32, (8, NZ), 1)
    row8 = lax.broadcasted_iota(jnp.int32, (8, NZ), 0)
    spread[...] = spread_now
    low_rows, high_rows = spread_now[0:8], spread_now[8:16]
    edges = jnp.where((lane8 < 32) | (lane8 >= 96), low_rows, pltpu.roll(high_rows, 64, 1))
    is_first = gy == 0
    side = jnp.where(is_first, high_rows, low_rows)
    used = row8 // HALO == 1 - gy
    side = jnp.where(used, side, misfit)
    for t in range(16):
        block[t, 0:8] = edges
        block[t, 8:16] = side
    for copy in copies:
        copy.wait()


def adjoint_kernel(adj, from_prev, from_next, from_side, coef_in, stored_in, *refs):
    spread, blocks, foot, owner, keep, away = refs[:6]
    coef, stored, elec, mag, inject, grad, sem = refs[6:]
    gx, gy = lax.axis_index("gx"), lax.axis_index("gy")
    tools = helpers(gy)
    lane, inside = tools[0], tools[1]

    copies = [
        pltpu.make_async_copy(adj.at[0, 0:3], elec.at[:, HALO : HALO + CX, 0:CY], sem.at[0]),
        pltpu.make_async_copy(adj.at[0, 3:6], mag.at[:, HALO : HALO + CX, 0:CY], sem.at[1]),
        pltpu.make_async_copy(coef_in, coef, sem.at[2]),
    ] + [
        pltpu.make_async_copy(stored_in.at[k], stored.at[k], sem.at[3 + k])
        for k in reversed(range(STEPS))
    ]
    for copy in copies:
        copy.start()
    zero_rows = jnp.zeros((HALO, NZ), F32)
    zero_plane = jnp.zeros((EY, NZ), F32)
    targets = [(elec, c) for c in range(3)] + [(mag, c) for c in range(3)]
    for c, (ref, index) in enumerate(targets):
        filled = set(range(HALO, HALO + CX))
        for source, planes, base in (
            (from_prev, ADJ_LOW, HALO - CX),
            (from_next, ADJ_HIGH, HALO + CX),
        ):
            for k, (comp, x) in enumerate(planes):
                if comp == c:
                    ref[index, x + base, 0:CY] = source[k]
                    filled.add(x + base)
        for i in range(EXP):
            if i not in filled:
                ref[index, i] = zero_plane

    row8 = lax.broadcasted_iota(jnp.int32, (8, NZ), 0)
    used = row8 // HALO == gy
    for k, dx in enumerate((-1, 0, 1)):
        there = (gx + dx >= 0) & (gx + dx < 8)
        near = jnp.clip(gx + dx, 0, 7)
        if dx == 0:
            inject[k, 0:16] = spread[...]
        else:
            edges = jnp.where(there, blocks[2 * near + gy, 0:8], 0.0)
            inject[k, 0:8] = edges
            inject[k, 8:16] = pltpu.roll(edges, 64, 1)
        side = blocks[2 * near + 1 - gy, 8:16]
        inject[k, 16:24] = jnp.where(used & there, side, 0.0)

    first = gy == 0
    for c, (ref, index) in enumerate(targets):
        for i in range(EX):
            rows = from_side[c, i]
            ref[index, i, CY : CY + HALO] = jnp.where(first, rows, zero_rows)
            ref[index, i, CY + HALO : EY] = jnp.where(first, zero_rows, rows)
    for copy in copies[:3]:
        copy.wait()

    at_depth = lane == ZREC

    for step in range(STEPS):
        when = STEPS - 1 - step

        for i in range(step, EX - step):
            source = inject[0 if i < HALO else 1 if i < HALO + CX else 2]
            x = (i - HALO) % CX
            for c in range(2):
                moved = pltpu.roll(source, (ZREC - (x * 8 + 2 * when + c)) % NZ, 1)
                elec[c, i] += jnp.where(at_depth, moved, 0.0)
        sweep(step, gx, elec, mag, coef, tools)

        copies[3 + step].wait()
        for x in range(CX):
            ax, ay, az = (elec[c, HALO + x, 0:CY] for c in range(3))
            horizontal = ax * stored[when, 0, x] + ay * stored[when, 1, x]
            vertical = az * stored[when, 2, x]
            if step:
                horizontal = grad[0, x] + horizontal
                vertical = grad[1, x] + vertical
            grad[0, x] = horizontal
            grad[1, x] = vertical

    flag = foot[0].astype(F32)
    misfit = blocks[0, 8:16][0:1]
    for t in range(1, 16):
        top = 0 if t % 2 == 0 else HALO
        misfit = misfit + blocks[t, 8:16][top : top + 1]
    core = lax.axis_index("tx") & 1
    for z in range(8):
        for ref, mine in ((keep, core), (away, 1 - core)):
            row = owner[2 * z + mine]
            ref[32 * z : 32 * z + 16] = grad[0, row] * flag
            ref[32 * z + 16 : 32 * z + 32] = grad[1, row] * flag
    keep[256:264] = jnp.broadcast_to(misfit, (8, NZ))
    away[256:264] = jnp.broadcast_to(misfit, (8, NZ))


def pair_kernel(mine, other, out):
    misfit = mine[256:264] + other[256:264]
    for z in range(8):
        out[z, 0:32] = mine[32 * z : 32 * z + 32] + other[32 * z : 32 * z + 32]
        out[z, 32:40] = misfit


def sum_kernel(blocks, part, misfit):
    total = blocks[0]
    for z in range(1, 8):
        total = total + blocks[z]
    part[0, 0, 0, 0] = total[0:16]
    part[0, 0, 1, 0] = total[16:32]
    misfit[...] = total[32:33, 0:1]


def on_device(cond_h, cond_v, fwd_init, adj_init, observed, footprint, owner, rec_cells):
    packed = pack(fwd_init, cond_h, cond_v, adj_init)
    to_next, to_prev, to_side, side_next, side_prev, adj_next, adj_prev = packed
    halos = (
        send(to_next, 1, False),
        send(to_prev, -1, False),
        send(to_side, 0, True),
        send(side_next, 1, True),
        send(side_prev, -1, True),
    )
    adj_halos = (send(adj_next, 1, False), send(adj_prev, -1, False))
    coef, stored, spread, block = pl.pallas_call(
        forward_kernel,
        out_shape=[
            pltpu.HBM((4, EXP, EY, NZ), F32),
            pltpu.HBM((STEPS, 3, CX, CY, NZ), F32),
            shape(CY, NZ),
            shape(16, 16, NZ),
        ],
        in_specs=[VMEM] * 10,
        out_specs=[HBM, HBM, VMEM, VMEM],
        scratch_shapes=[
            pltpu.VMEM((4, EXP, EY, NZ), F32),
            pltpu.VMEM((STEPS, 3, CX, CY, NZ), F32),
            pltpu.VMEM((3, EXP, EY, NZ), F32),
            pltpu.VMEM((3, EXP, EY, NZ), F32),
            pltpu.SemaphoreType.DMA((STEPS + 1,)),
        ],
        compiler_params=params(),
        name="forward",
    )(fwd_init, cond_h, cond_v, *halos, observed.reshape(8, 32), rec_cells.reshape(1, 32))
    block, *adj_ready = lax.optimization_barrier((block, *adj_halos))
    adj_side = pl.pallas_call(
        pack_side_kernel,
        out_shape=shape(6, EX, HALO, NZ),
        in_specs=[VMEM] * 3,
        out_specs=VMEM,
        compiler_params=params(),
        name="pack_side",
    )(adj_init, *adj_ready)
    block, adj_side = lax.optimization_barrier((block, adj_side))
    from_side = send(adj_side, 0, True)
    blocks = lax.all_to_all(block, ("gx", "gy"), 0, 0, tiled=True)
    keep, away = pl.pallas_call(
        adjoint_kernel,
        out_shape=[shape(264, NZ)] * 2,
        in_specs=[HBM] + [VMEM] * 3 + [HBM] * 2 + [VMEM] * 2 + [SMEM, SMEM],
        out_specs=[VMEM] * 2,
        scratch_shapes=[
            pltpu.VMEM((4, EXP, EY, NZ), F32),
            pltpu.VMEM((STEPS, 3, CX, CY, NZ), F32),
            pltpu.VMEM((3, EXP, EY, NZ), F32),
            pltpu.VMEM((3, EXP, EY, NZ), F32),
            pltpu.VMEM((3, EY, NZ), F32),
            pltpu.VMEM((2, CX, CY, NZ), F32),
            pltpu.SemaphoreType.DMA((3 + STEPS,)),
        ],
        compiler_params=params(),
        name="adjoint",
    )(
        in_hbm(adj_init),
        *adj_halos,
        from_side,
        in_hbm(coef),
        in_hbm(stored),
        spread,
        blocks,
        footprint.reshape(1),
        owner.reshape(16),
    )
    size = lax.axis_size("tx")
    other = lax.ppermute(away, "tx", [(t, t ^ 1) for t in range(size)])
    paired = pl.pallas_call(
        pair_kernel,
        out_shape=shape(8, 40, NZ),
        in_specs=[VMEM] * 2,
        out_specs=VMEM,
        compiler_params=params(),
        name="pair",
    )(keep, other)
    along_z = [list(range(core, size, 2)) for core in range(2)]
    summed = lax.all_to_all(paired, "tx", 0, 0, axis_index_groups=along_z, tiled=True)
    part, misfit = pl.pallas_call(
        sum_kernel,
        out_shape=[shape(1, 1, 2, 1, CY, NZ), shape(1, 1)],
        in_specs=[VMEM],
        out_specs=[VMEM, VMEM],
        compiler_params=params(),
        name="total",
    )(summed)
    return part, misfit.reshape(())


def solution(mesh):
    placed = (
        P("gx", "gy", None),
        P("gx", "gy", None),
        P("tx", None, "gx", "gy", None),
        P("tx", None, "gx", "gy", None),
        P("tx", None, "gx", "gy", None, None),
        P("tx", "gx", "gy"),
        P("gx", "gy", None),
        P("gx", "gy", None),
    )
    return jax.shard_map(
        on_device,
        mesh=mesh,
        in_specs=placed,
        out_specs=(P("gx", "tx", None, None, "gy", None), P()),
        check_vma=False,
    )
```

```python
import jax
import jax.numpy as jnp
from jax import lax
from jax.experimental import pallas as pl
from jax.experimental.pallas import tpu as pltpu
from jax.sharding import PartitionSpec as P

STEPS = 4
ZREC = 32
STEP_DT = 0.5
HALO = 4
CX = 16
CY = 16
NZ = 128
EX = CX + 2 * HALO
EXP = EX + 4
EY = CY + 2 * HALO
F32 = jnp.float32
HIGHEST = lax.Precision.HIGHEST

LOW = [(c, x) for c in range(8) for x in range(CX - HALO + (c in (3, 6, 7)), CX)]
HIGH = [(c, x) for c in range(8) for x in range(HALO - (c not in (1, 2)))]
ADJ_LOW = [(c, x) for c, x in LOW if c < 6]
ADJ_HIGH = [(c, x) for c, x in HIGH if c < 6]
VMEM = pl.BlockSpec(memory_space=pltpu.VMEM)
SMEM = pl.BlockSpec(memory_space=pltpu.SMEM)
HBM = pl.BlockSpec(memory_space=pltpu.HBM)


def shape(*dims):
    return jax.ShapeDtypeStruct(dims, F32)


def in_hbm(array):
    return pltpu.with_memory_space_constraint(array, pltpu.HBM)


def params():
    return pltpu.CompilerParams(vmem_limit_bytes=8 * 1024 * 1024)


def plane_of(refs, comp, x):
    return refs[0][0, comp, x] if comp < 6 else refs[comp - 5][x]


def edge_of(plane, second):
    return jnp.where(second, plane[0:HALO], plane[CY - HALO : CY])


def pack_kernel(fwd, cond_h, cond_v, adj, *refs):
    to_next, to_prev, to_side, side_next, side_prev, adj_side = refs[:6]
    bufs, sem = refs[6:10], refs[10]
    copies = [
        pltpu.make_async_copy(src, dst, sem.at[k])
        for k, (src, dst) in enumerate(zip((fwd, cond_h, cond_v, adj), bufs))
    ]
    for copy in copies:
        copy.start()
    second = lax.axis_index("gy") == 1
    for which, comps in ((0, range(6)), (1, (6,)), (2, (7,))):
        copies[which].wait()
        for c in comps:
            edges = [edge_of(plane_of(bufs, c, x), second) for x in range(CX)]
            for x in range(CX):
                to_side[c, x] = edges[x]
            for k, (comp, x) in enumerate(LOW):
                if comp == c:
                    to_next[k] = plane_of(bufs, c, x)
                    side_next[k] = edges[x]
            for k, (comp, x) in enumerate(HIGH):
                if comp == c:
                    to_prev[k] = plane_of(bufs, c, x)
                    side_prev[k] = edges[x]
    copies[3].wait()
    for c in range(6):
        edges = [edge_of(bufs[3][0, c, x], second) for x in range(CX)]
        for x in range(CX):
            adj_side[c, x] = edges[x]
        for k, (comp, x) in enumerate(ADJ_LOW):
            if comp == c:
                to_next[len(LOW) + k] = bufs[3][0, c, x]
                side_next[len(LOW) + k] = edges[x]
        for k, (comp, x) in enumerate(ADJ_HIGH):
            if comp == c:
                to_prev[len(HIGH) + k] = bufs[3][0, c, x]
                side_prev[len(HIGH) + k] = edges[x]


def pack(*arrays):
    return pl.pallas_call(
        pack_kernel,
        out_shape=[
            shape(len(LOW) + len(ADJ_LOW), CY, NZ),
            shape(len(HIGH) + len(ADJ_HIGH), CY, NZ),
            shape(8, CX, HALO, NZ),
            shape(len(LOW) + len(ADJ_LOW), HALO, NZ),
            shape(len(HIGH) + len(ADJ_HIGH), HALO, NZ),
            shape(6, CX, HALO, NZ),
        ],
        in_specs=[HBM] * 4,
        out_specs=[VMEM] * 6,
        scratch_shapes=[pltpu.VMEM(a.shape, F32) for a in arrays]
        + [pltpu.SemaphoreType.DMA((4,))],
        compiler_params=params(),
        name="pack",
    )(*(in_hbm(a) for a in arrays))


def pairs(dx, swap):
    size_x = lax.axis_size("gx")
    size_y = lax.axis_size("gy")
    return [
        (x * size_y + y, (x + dx) * size_y + (1 - y if swap else y))
        for x in range(size_x)
        for y in range(size_y)
        if 0 <= x + dx < size_x
    ]


def send(array, dx, swap):
    return lax.ppermute(array, ("gx", "gy"), pairs(dx, swap))


def assemble(own, halos, comps, first):
    from_prev, from_next, from_side, side_prev, side_next = halos
    zero_rows = jnp.zeros((HALO, NZ), F32)
    zero_plane = jnp.zeros((EY, NZ), F32)

    def put(ref, index, i, plane, rows):
        ref[index, i, 0:CY] = plane
        ref[index, i, CY : CY + HALO] = jnp.where(first, rows, zero_rows)
        ref[index, i, CY + HALO : EY] = jnp.where(first, zero_rows, rows)

    for c, (ref, index) in comps.items():
        filled = set()
        for x in range(CX):
            put(ref, index, HALO + x, own(c, x), from_side[c, x])
            filled.add(HALO + x)
        for k, (comp, x) in enumerate(LOW):
            if comp == c:
                i = x - (CX - HALO)
                put(ref, index, i, from_prev[k], side_prev[k])
                filled.add(i)
        for k, (comp, x) in enumerate(HIGH):
            if comp == c:
                i = x + HALO + CX
                put(ref, index, i, from_next[k], side_next[k])
                filled.add(i)
        for i in range(EXP):
            if i not in filled:
                ref[index, i] = zero_plane


def helpers(gy):
    lane = lax.broadcasted_iota(jnp.int32, (EY, NZ), 1)
    row = lax.broadcasted_iota(jnp.int32, (EY, NZ), 0)
    y = jnp.where(row < CY + HALO, row, row - EY) + gy * CY
    inside = (y >= 0) & (y < 2 * CY)
    last, start = lane == NZ - 1, lane == 0

    def z_up(f):
        return jnp.where(last, 0.0, pltpu.roll(f, NZ - 1, 1))

    def z_down(f):
        return jnp.where(start, 0.0, pltpu.roll(f, 1, 1))

    def y_up(f):
        return pltpu.roll(f, EY - 1, 0)

    def y_down(f):
        return pltpu.roll(f, 1, 0)

    return lane, inside, z_up, z_down, y_up, y_down


def in_grid(gx, i):
    x = gx * CX + i - HALO
    return (x >= 0) & (x < 8 * CX)


UNROLL = 24


def sweep(step, gx, elec, mag, coef, tools):
    _, inside, z_up, z_down, y_up, y_down = tools
    half = jnp.where(inside, STEP_DT, 0.0)
    zero = jnp.zeros((EY, NZ), F32)
    count = EX - 1 - 2 * step
    unroll = min(UNROLL, count)
    turns = -(-count // unroll)

    def magnetic(i, field, after):
        ex, ey, ez = field
        _, ey_next, ez_next = after
        rate = jnp.where(in_grid(gx, i), half, zero)
        hx = mag[0, i] - rate * ((y_up(ez) - ez) - (z_up(ey) - ey))
        hy = mag[1, i] - rate * ((z_up(ex) - ex) - (ez_next - ez))
        hz = mag[2, i] - rate * ((ey_next - ey) - (y_up(ex) - ex))
        return hx, hy, hz

    def electric(i, field, now, before):
        ex, ey, ez = field
        hx, hy, hz = now
        decay_h, drive_h, decay_v, drive_v = (coef[k, i] for k in range(4))
        ex = decay_h * ex + drive_h * ((hz - y_down(hz)) - (hy - z_down(hy)))
        ey = decay_h * ey + drive_h * ((hx - z_down(hx)) - (hz - before[2]))
        ez = decay_v * ez + drive_v * ((hy - before[1]) - (hx - y_down(hx)))
        return ex, ey, ez

    def planes(ref, i, n):
        return [tuple(ref[c, i + k] for c in range(3)) for k in range(n)]

    def put(ref, i, values):
        for k, plane in enumerate(values):
            for c in range(3):
                ref[c, i + k] = plane[c]

    def body(turn, carry):
        i = step + turn * unroll
        field = planes(elec, i, unroll + 1)
        now = [magnetic(i + k, field[k], field[k + 1]) for k in range(unroll)]
        put(mag, i, now)
        before = [(None, *carry)] + now[:-1]
        put(elec, i, [electric(i + k, field[k], now[k], before[k]) for k in range(unroll)])
        return now[-1][1:]

    if turns == 1:
        body(0, (zero, zero))
    else:
        lax.fori_loop(0, turns, body, (zero, zero))


def dot(a, b, dim_a, dim_b):
    dims = (((dim_a,), (dim_b,)), ((), ()))
    return lax.dot_general(a, b, dims, precision=HIGHEST, preferred_element_type=F32)


def forward_kernel(fwd, cond_h, cond_v, *refs):
    halos, refs = refs[:5], refs[5:]
    observed, rec_vec, coef_out, stored_out, spread, block = refs[:6]
    adj_halos, refs = refs[6:10], refs[10:]
    coef, stored, elec, mag, sem = refs
    gx, gy = lax.axis_index("gx"), lax.axis_index("gy")
    tools = helpers(gy)
    lane, inside = tools[0], tools[1]

    adjoint_part = (halos[0].at[len(LOW) :], halos[1].at[len(HIGH) :])
    adjoint_part += (halos[3].at[len(LOW) :], halos[4].at[len(HIGH) :])
    copies = [
        pltpu.make_async_copy(src, dst, sem.at[STEPS + 1 + k])
        for k, (src, dst) in enumerate(zip(adjoint_part, adj_halos))
    ]
    for copy in copies:
        copy.start()
    comps = {c: (elec, c) if c < 3 else (mag, c - 3) for c in range(6)}
    comps |= {6: (coef, 0), 7: (coef, 2)}
    assemble(lambda c, x: plane_of((fwd, cond_h, cond_v, None), c, x), halos, comps, gy == 0)

    def coefficients(turn, carry):
        for i in [turn * 8 + k for k in range(8)]:
            keep = inside & in_grid(gx, i)
            for k in (0, 2):
                half_rate = 0.25 * coef[k, i]
                inverse = 1.0 / (1.0 + half_rate)
                coef[k, i] = jnp.where(keep, (1.0 - half_rate) * inverse, 0.0)
                coef[k + 1, i] = jnp.where(keep, STEP_DT * inverse, 0.0)
        return carry

    lax.fori_loop(0, EX // 8, coefficients, 0)
    for k in (1, 3):
        coef[k, EX:EXP] = jnp.zeros((EXP - EX, EY, NZ), F32)

    cells = rec_vec[...]
    at_y = ((cells & 15) == lax.broadcasted_iota(jnp.int32, (CY, 32), 0)).astype(F32)
    cell_x = ((cells >> 4) == lax.broadcasted_iota(jnp.int32, (CX, 32), 0)).astype(F32)
    lane_x = lax.broadcasted_iota(jnp.int32, (CX, NZ), 1) >> 3
    lane_q = lax.broadcasted_iota(jnp.int32, (8, NZ), 1) & 7
    at_x = dot(cell_x, (lane_x == lax.broadcasted_iota(jnp.int32, (CX, NZ), 0)).astype(F32), 0, 0)
    target = dot(
        observed[...], (lane_q == lax.broadcasted_iota(jnp.int32, (8, NZ), 0)).astype(F32), 0, 0
    )
    copies.append(pltpu.make_async_copy(coef, coef_out, sem.at[STEPS]))
    copies[-1].start()
    for step in range(STEPS):
        sweep(step, gx, elec, mag, coef, tools)
        stored[step] = elec[:, HALO : HALO + CX, 0:CY]
        copies.append(pltpu.make_async_copy(stored.at[step], stored_out.at[step], sem.at[step]))
        copies[-1].start()

    at_depth = lane[0:CY] == ZREC
    record = jnp.zeros((CY, NZ), F32)
    for x in range(CX):
        for q in range(8):
            column = jnp.where(at_depth, stored[q // 2, q % 2, x], 0.0)
            record = record + pltpu.roll(column, (x * 8 + q - ZREC) % NZ, 1)
    at_receivers = dot(at_y, record, 0, 0)
    residual = at_x * (at_receivers - target)
    misfit = 0.5 * jnp.sum(residual * residual)
    spread_now = dot(at_y, residual, 1, 0)
    lane8 = lax.broadcasted_iota(jnp.int32, (8, NZ), 1)
    row8 = lax.broadcasted_iota(jnp.int32, (8, NZ), 0)
    spread[...] = spread_now
    low_rows, high_rows = spread_now[0:8], spread_now[8:16]
    edges = jnp.where((lane8 < 32) | (lane8 >= 96), low_rows, pltpu.roll(high_rows, 64, 1))
    is_first = gy == 0
    side = jnp.where(is_first, high_rows, low_rows)
    used = row8 // HALO == 1 - gy
    side = jnp.where(used, side, misfit)
    for t in range(16):
        block[t, 0:8] = edges
        block[t, 8:16] = side
    for copy in copies:
        copy.wait()


def adjoint_kernel(adj, from_prev, from_next, corner_prev, corner_next, from_side, *refs):
    coef_in, stored_in, spread, blocks, foot, owner, keep, away = refs[:8]
    coef, stored, elec, mag, corner_low, corner_high, inject, grad, sem = refs[8:]
    gx, gy = lax.axis_index("gx"), lax.axis_index("gy")
    tools = helpers(gy)
    lane, inside = tools[0], tools[1]

    own = slice(HALO, HALO + CX)
    moves = [
        (corner_prev, corner_low),
        (corner_next, corner_high),
        (adj.at[0, 0:3], elec.at[:, own, 0:CY]),
        (adj.at[0, 3:6], mag.at[:, own, 0:CY]),
    ]
    targets = [(elec, c) for c in range(3)] + [(mag, c) for c in range(3)]
    sides = (
        (from_prev, corner_low, ADJ_LOW, HALO - CX),
        (from_next, corner_high, ADJ_HIGH, HALO + CX),
    )
    for c, (ref, index) in enumerate(targets):
        for source, _, planes, base in sides:
            ks = [k for k, (comp, _) in enumerate(planes) if comp == c]
            i = planes[ks[0]][1] + base
            moves.append(
                (source.at[ks[0] : ks[-1] + 1], ref.at[index, i : i + len(ks), 0:CY])
            )
    moves.append((coef_in, coef))
    moves += [(stored_in.at[k], stored.at[k]) for k in reversed(range(STEPS))]
    copies = [
        pltpu.make_async_copy(src, dst, sem.at[k]) for k, (src, dst) in enumerate(moves)
    ]
    for copy in copies:
        copy.start()

    row8 = lax.broadcasted_iota(jnp.int32, (8, NZ), 0)
    used = row8 // HALO == gy
    for k, dx in enumerate((-1, 0, 1)):
        there = (gx + dx >= 0) & (gx + dx < 8)
        near = jnp.clip(gx + dx, 0, 7)
        if dx == 0:
            inject[k, 0:16] = spread[...]
        else:
            edges = jnp.where(there, blocks[2 * near + gy, 0:8], 0.0)
            inject[k, 0:8] = edges
            inject[k, 8:16] = pltpu.roll(edges, 64, 1)
        side = blocks[2 * near + 1 - gy, 8:16]
        inject[k, 16:24] = jnp.where(used & there, side, 0.0)

    first = gy == 0
    zero_rows = jnp.zeros((HALO, NZ), F32)
    zero_plane = jnp.zeros((EY, NZ), F32)

    def put_rows(ref, index, i, rows):
        ref[index, i, CY : CY + HALO] = jnp.where(first, rows, zero_rows)
        ref[index, i, CY + HALO : EY] = jnp.where(first, zero_rows, rows)

    for c, (ref, index) in enumerate(targets):
        for x in range(CX):
            put_rows(ref, index, HALO + x, from_side[c, x])
    for copy in copies[:2]:
        copy.wait()
    for c, (ref, index) in enumerate(targets):
        filled = set(range(HALO, HALO + CX))
        for _, corner, planes, base in sides:
            for k, (comp, x) in enumerate(planes):
                if comp == c:
                    put_rows(ref, index, x + base, corner[k])
                    filled.add(x + base)
        for i in range(EXP):
            if i not in filled:
                ref[index, i] = zero_plane
    for copy in copies[2:-STEPS]:
        copy.wait()

    at_depth = lane == ZREC

    for step in range(STEPS):
        when = STEPS - 1 - step

        for i in range(step, EX - step):
            source = inject[0 if i < HALO else 1 if i < HALO + CX else 2]
            x = (i - HALO) % CX
            for c in range(2):
                moved = pltpu.roll(source, (ZREC - (x * 8 + 2 * when + c)) % NZ, 1)
                elec[c, i] += jnp.where(at_depth, moved, 0.0)
        sweep(step, gx, elec, mag, coef, tools)

        copies[step - STEPS].wait()
        for x in range(CX):
            ax, ay, az = (elec[c, HALO + x, 0:CY] for c in range(3))
            horizontal = ax * stored[when, 0, x] + ay * stored[when, 1, x]
            vertical = az * stored[when, 2, x]
            if step:
                horizontal = grad[0, x] + horizontal
                vertical = grad[1, x] + vertical
            grad[0, x] = horizontal
            grad[1, x] = vertical

    flag = foot[0].astype(F32)
    misfit = blocks[0, 8:16][0:1]
    for t in range(1, 16):
        top = 0 if t % 2 == 0 else HALO
        misfit = misfit + blocks[t, 8:16][top : top + 1]
    core = lax.axis_index("tx") & 1
    for z in range(8):
        for ref, mine in ((keep, core), (away, 1 - core)):
            row = owner[2 * z + mine]
            ref[32 * z : 32 * z + 16] = grad[0, row] * flag
            ref[32 * z + 16 : 32 * z + 32] = grad[1, row] * flag
    keep[256:264] = jnp.broadcast_to(misfit, (8, NZ))
    away[256:264] = jnp.broadcast_to(misfit, (8, NZ))


def pair_kernel(mine, other, out):
    misfit = mine[256:264] + other[256:264]
    for z in range(8):
        out[z, 0:32] = mine[32 * z : 32 * z + 32] + other[32 * z : 32 * z + 32]
        out[z, 32:40] = misfit


def sum_kernel(blocks, part, misfit):
    total = blocks[0]
    for z in range(1, 8):
        total = total + blocks[z]
    part[0, 0, 0, 0] = total[0:16]
    part[0, 0, 1, 0] = total[16:32]
    misfit[...] = total[32:33, 0:1]


def on_device(cond_h, cond_v, fwd_init, adj_init, observed, footprint, owner, rec_cells):
    packed = pack(fwd_init, cond_h, cond_v, adj_init)
    to_next, to_prev, to_side, side_next, side_prev, adj_side = packed
    halos = (
        send(to_next, 1, False),
        send(to_prev, -1, False),
        send(to_side, 0, True),
        send(side_next, 1, True),
        send(side_prev, -1, True),
    )
    from_side = send(adj_side, 0, True)
    coef, stored, spread, block, *adj_halos = pl.pallas_call(
        forward_kernel,
        out_shape=[
            pltpu.HBM((4, EXP, EY, NZ), F32),
            pltpu.HBM((STEPS, 3, CX, CY, NZ), F32),
            shape(CY, NZ),
            shape(16, 16, NZ),
            pltpu.HBM((len(ADJ_LOW), CY, NZ), F32),
            pltpu.HBM((len(ADJ_HIGH), CY, NZ), F32),
            pltpu.HBM((len(ADJ_LOW), HALO, NZ), F32),
            pltpu.HBM((len(ADJ_HIGH), HALO, NZ), F32),
        ],
        in_specs=[VMEM] * 10,
        out_specs=[HBM, HBM, VMEM, VMEM] + [HBM] * 4,
        scratch_shapes=[
            pltpu.VMEM((4, EXP, EY, NZ), F32),
            pltpu.VMEM((STEPS, 3, CX, CY, NZ), F32),
            pltpu.VMEM((3, EXP, EY, NZ), F32),
            pltpu.VMEM((3, EXP, EY, NZ), F32),
            pltpu.SemaphoreType.DMA((STEPS + 5,)),
        ],
        compiler_params=params(),
        name="forward",
    )(fwd_init, cond_h, cond_v, *halos, observed.reshape(8, 32), rec_cells.reshape(1, 32))
    blocks = lax.all_to_all(block, ("gx", "gy"), 0, 0, tiled=True)
    keep, away = pl.pallas_call(
        adjoint_kernel,
        out_shape=[shape(264, NZ)] * 2,
        in_specs=[HBM] * 5 + [VMEM] + [HBM] * 2 + [VMEM] * 2 + [SMEM, SMEM],
        out_specs=[VMEM] * 2,
        scratch_shapes=[
            pltpu.VMEM((4, EXP, EY, NZ), F32),
            pltpu.VMEM((STEPS, 3, CX, CY, NZ), F32),
            pltpu.VMEM((3, EXP, EY, NZ), F32),
            pltpu.VMEM((3, EXP, EY, NZ), F32),
            pltpu.VMEM((len(ADJ_LOW), HALO, NZ), F32),
            pltpu.VMEM((len(ADJ_HIGH), HALO, NZ), F32),
            pltpu.VMEM((3, EY, NZ), F32),
            pltpu.VMEM((2, CX, CY, NZ), F32),
            pltpu.SemaphoreType.DMA((17 + STEPS,)),
        ],
        compiler_params=params(),
        name="adjoint",
    )(
        in_hbm(adj_init),
        *(in_hbm(halo) for halo in adj_halos),
        from_side,
        in_hbm(coef),
        in_hbm(stored),
        spread,
        blocks,
        footprint.reshape(1),
        owner.reshape(16),
    )
    size = lax.axis_size("tx")
    other = lax.ppermute(away, "tx", [(t, t ^ 1) for t in range(size)])
    paired = pl.pallas_call(
        pair_kernel,
        out_shape=shape(8, 40, NZ),
        in_specs=[VMEM] * 2,
        out_specs=VMEM,
        compiler_params=params(),
        name="pair",
    )(keep, other)
    along_z = [list(range(core, size, 2)) for core in range(2)]
    summed = lax.all_to_all(paired, "tx", 0, 0, axis_index_groups=along_z, tiled=True)
    part, misfit = pl.pallas_call(
        sum_kernel,
        out_shape=[shape(1, 1, 2, 1, CY, NZ), shape(1, 1)],
        in_specs=[VMEM],
        out_specs=[VMEM, VMEM],
        compiler_params=params(),
        name="total",
    )(summed)
    return part, misfit.reshape(())


def solution(mesh):
    placed = (
        P("gx", "gy", None),
        P("gx", "gy", None),
        P("tx", None, "gx", "gy", None),
        P("tx", None, "gx", "gy", None),
        P("tx", None, "gx", "gy", None, None),
        P("tx", "gx", "gy"),
        P("gx", "gy", None),
        P("gx", "gy", None),
    )
    return jax.shard_map(
        on_device,
        mesh=mesh,
        in_specs=placed,
        out_specs=(P("gx", "tx", None, None, "gy", None), P()),
        check_vma=False,
    )
```

```python
import jax
import jax.numpy as jnp
from jax import lax
from jax.experimental import pallas as pl
from jax.experimental.pallas import tpu as pltpu
from jax.sharding import PartitionSpec as P

STEPS = 4
ZREC = 32
STEP_DT = 0.5
HALO = 4
CX = 16
CY = 16
NZ = 128
EX = CX + 2 * HALO
EXP = EX + 4
EY = CY + 2 * HALO
F32 = jnp.float32
HIGHEST = lax.Precision.HIGHEST

LOW = [(c, x) for c in range(8) for x in range(CX - HALO + (c in (3, 6, 7)), CX)]
HIGH = [(c, x) for c in range(8) for x in range(HALO - (c not in (1, 2)))]
ADJ_LOW = [(c, x) for c, x in LOW if c < 6]
ADJ_HIGH = [(c, x) for c, x in HIGH if c < 6]
VMEM = pl.BlockSpec(memory_space=pltpu.VMEM)
SMEM = pl.BlockSpec(memory_space=pltpu.SMEM)
HBM = pl.BlockSpec(memory_space=pltpu.HBM)


def shape(*dims):
    return jax.ShapeDtypeStruct(dims, F32)


def in_hbm(array):
    return pltpu.with_memory_space_constraint(array, pltpu.HBM)


def params():
    return pltpu.CompilerParams(vmem_limit_bytes=8 * 1024 * 1024)


def plane_of(refs, comp, x):
    return refs[0][0, comp, x] if comp < 6 else refs[comp - 5][x]


def edge_of(plane, second):
    return jnp.where(second, plane[0:HALO], plane[CY - HALO : CY])


def pack_adjoint_kernel(adj, to_next, to_prev, sem):
    copies = []
    for ref, planes in ((to_next, ADJ_LOW), (to_prev, ADJ_HIGH)):
        for c in range(6):
            ks = [k for k, (comp, _) in enumerate(planes) if comp == c]
            x = planes[ks[0]][1]
            src, dst = adj.at[0, c, x : x + len(ks)], ref.at[ks[0] : ks[-1] + 1]
            copies.append(pltpu.make_async_copy(src, dst, sem.at[len(copies)]))
    for copy in copies:
        copy.start()
    for copy in copies:
        copy.wait()


def pack_adjoint(adj):
    return pl.pallas_call(
        pack_adjoint_kernel,
        out_shape=[shape(len(ADJ_LOW), CY, NZ), shape(len(ADJ_HIGH), CY, NZ)],
        in_specs=[HBM],
        out_specs=[VMEM] * 2,
        scratch_shapes=[pltpu.SemaphoreType.DMA((12,))],
        compiler_params=params(),
        name="pack_adjoint",
    )(in_hbm(adj))


def pack_kernel(fwd, cond_h, cond_v, *refs):
    to_next, to_prev, to_side, side_next, side_prev = refs[:5]
    bufs, sem = refs[5:8], refs[8]
    copies = [
        pltpu.make_async_copy(src, dst, sem.at[k])
        for k, (src, dst) in enumerate(zip((fwd, cond_h, cond_v), bufs))
    ]
    for copy in copies:
        copy.start()
    second = lax.axis_index("gy") == 1
    for which, comps in ((0, range(6)), (1, (6,)), (2, (7,))):
        copies[which].wait()
        for c in comps:
            edges = [edge_of(plane_of(bufs, c, x), second) for x in range(CX)]
            for x in range(CX):
                to_side[c, x] = edges[x]
            for k, (comp, x) in enumerate(LOW):
                if comp == c:
                    to_next[k] = plane_of(bufs, c, x)
                    side_next[k] = edges[x]
            for k, (comp, x) in enumerate(HIGH):
                if comp == c:
                    to_prev[k] = plane_of(bufs, c, x)
                    side_prev[k] = edges[x]


def pack(*arrays):
    return pl.pallas_call(
        pack_kernel,
        out_shape=[
            shape(len(LOW), CY, NZ),
            shape(len(HIGH), CY, NZ),
            shape(8, CX, HALO, NZ),
            shape(len(LOW), HALO, NZ),
            shape(len(HIGH), HALO, NZ),
        ],
        in_specs=[HBM] * 3,
        out_specs=[VMEM] * 5,
        scratch_shapes=[pltpu.VMEM(a.shape, F32) for a in arrays]
        + [pltpu.SemaphoreType.DMA((3,))],
        compiler_params=params(),
        name="pack",
    )(*(in_hbm(a) for a in arrays))


def pack_side_kernel(adj, from_prev, from_next, to_side):
    second = lax.axis_index("gy") == 1
    for c in range(6):
        for x in range(CX):
            to_side[c, HALO + x] = edge_of(adj[0, c, x], second)
        filled = set(range(HALO, HALO + CX))
        for k, (comp, x) in enumerate(ADJ_LOW):
            if comp == c:
                to_side[c, x - (CX - HALO)] = edge_of(from_prev[k], second)
                filled.add(x - (CX - HALO))
        for k, (comp, x) in enumerate(ADJ_HIGH):
            if comp == c:
                to_side[c, x + HALO + CX] = edge_of(from_next[k], second)
                filled.add(x + HALO + CX)
        for i in range(EX):
            if i not in filled:
                to_side[c, i] = jnp.zeros((HALO, NZ), F32)


def pairs(dx, swap):
    size_x = lax.axis_size("gx")
    size_y = lax.axis_size("gy")
    return [
        (x * size_y + y, (x + dx) * size_y + (1 - y if swap else y))
        for x in range(size_x)
        for y in range(size_y)
        if 0 <= x + dx < size_x
    ]


def send(array, dx, swap):
    return lax.ppermute(array, ("gx", "gy"), pairs(dx, swap))


def assemble(own, halos, comps, first):
    from_prev, from_next, from_side, side_prev, side_next = halos
    zero_rows = jnp.zeros((HALO, NZ), F32)
    zero_plane = jnp.zeros((EY, NZ), F32)

    def put(ref, index, i, plane, rows):
        ref[index, i, 0:CY] = plane
        ref[index, i, CY : CY + HALO] = jnp.where(first, rows, zero_rows)
        ref[index, i, CY + HALO : EY] = jnp.where(first, zero_rows, rows)

    for c, (ref, index) in comps.items():
        filled = set()
        for x in range(CX):
            put(ref, index, HALO + x, own(c, x), from_side[c, x])
            filled.add(HALO + x)
        for k, (comp, x) in enumerate(LOW):
            if comp == c:
                i = x - (CX - HALO)
                put(ref, index, i, from_prev[k], side_prev[k])
                filled.add(i)
        for k, (comp, x) in enumerate(HIGH):
            if comp == c:
                i = x + HALO + CX
                put(ref, index, i, from_next[k], side_next[k])
                filled.add(i)
        for i in range(EXP):
            if i not in filled:
                ref[index, i] = zero_plane


def helpers(gy):
    lane = lax.broadcasted_iota(jnp.int32, (EY, NZ), 1)
    row = lax.broadcasted_iota(jnp.int32, (EY, NZ), 0)
    y = jnp.where(row < CY + HALO, row, row - EY) + gy * CY
    inside = (y >= 0) & (y < 2 * CY)
    last, start = lane == NZ - 1, lane == 0

    def z_up(f):
        return jnp.where(last, 0.0, pltpu.roll(f, NZ - 1, 1))

    def z_down(f):
        return jnp.where(start, 0.0, pltpu.roll(f, 1, 1))

    def y_up(f):
        return pltpu.roll(f, EY - 1, 0)

    def y_down(f):
        return pltpu.roll(f, 1, 0)

    return lane, inside, z_up, z_down, y_up, y_down


def in_grid(gx, i):
    x = gx * CX + i - HALO
    return (x >= 0) & (x < 8 * CX)


UNROLL = 24


def sweep(step, gx, elec, mag, coef, tools):
    _, inside, z_up, z_down, y_up, y_down = tools
    half = jnp.where(inside, STEP_DT, 0.0)
    zero = jnp.zeros((EY, NZ), F32)
    count = EX - 1 - 2 * step
    unroll = min(UNROLL, count)
    turns = -(-count // unroll)

    def magnetic(i, field, after):
        ex, ey, ez = field
        _, ey_next, ez_next = after
        rate = jnp.where(in_grid(gx, i), half, zero)
        hx = mag[0, i] - rate * ((y_up(ez) - ez) - (z_up(ey) - ey))
        hy = mag[1, i] - rate * ((z_up(ex) - ex) - (ez_next - ez))
        hz = mag[2, i] - rate * ((ey_next - ey) - (y_up(ex) - ex))
        return hx, hy, hz

    def electric(i, field, now, before):
        ex, ey, ez = field
        hx, hy, hz = now
        decay_h, drive_h, decay_v, drive_v = (coef[k, i] for k in range(4))
        ex = decay_h * ex + drive_h * ((hz - y_down(hz)) - (hy - z_down(hy)))
        ey = decay_h * ey + drive_h * ((hx - z_down(hx)) - (hz - before[2]))
        ez = decay_v * ez + drive_v * ((hy - before[1]) - (hx - y_down(hx)))
        return ex, ey, ez

    def planes(ref, i, n):
        return [tuple(ref[c, i + k] for c in range(3)) for k in range(n)]

    def put(ref, i, values):
        for k, plane in enumerate(values):
            for c in range(3):
                ref[c, i + k] = plane[c]

    def body(turn, carry):
        i = step + turn * unroll
        field = planes(elec, i, unroll + 1)
        now = [magnetic(i + k, field[k], field[k + 1]) for k in range(unroll)]
        put(mag, i, now)
        before = [(None, *carry)] + now[:-1]
        put(elec, i, [electric(i + k, field[k], now[k], before[k]) for k in range(unroll)])
        return now[-1][1:]

    if turns == 1:
        body(0, (zero, zero))
    else:
        lax.fori_loop(0, turns, body, (zero, zero))


def dot(a, b, dim_a, dim_b):
    dims = (((dim_a,), (dim_b,)), ((), ()))
    return lax.dot_general(a, b, dims, precision=HIGHEST, preferred_element_type=F32)


def forward_kernel(fwd, cond_h, cond_v, *refs):
    halos, refs = refs[:5], refs[5:]
    observed, rec_vec, coef_out, stored_out, spread, block = refs[:6]
    coef, stored, elec, mag, sem = refs[6:]
    gx, gy = lax.axis_index("gx"), lax.axis_index("gy")
    tools = helpers(gy)
    lane, inside = tools[0], tools[1]

    comps = {c: (elec, c) if c < 3 else (mag, c - 3) for c in range(6)}
    comps |= {6: (coef, 0), 7: (coef, 2)}
    assemble(lambda c, x: plane_of((fwd, cond_h, cond_v, None), c, x), halos, comps, gy == 0)

    def coefficients(turn, carry):
        for i in [turn * 8 + k for k in range(8)]:
            keep = inside & in_grid(gx, i)
            for k in (0, 2):
                half_rate = 0.25 * coef[k, i]
                inverse = 1.0 / (1.0 + half_rate)
                coef[k, i] = jnp.where(keep, (1.0 - half_rate) * inverse, 0.0)
                coef[k + 1, i] = jnp.where(keep, STEP_DT * inverse, 0.0)
        return carry

    lax.fori_loop(0, EX // 8, coefficients, 0)
    for k in (1, 3):
        coef[k, EX:EXP] = jnp.zeros((EXP - EX, EY, NZ), F32)

    cells = rec_vec[...]
    at_y = ((cells & 15) == lax.broadcasted_iota(jnp.int32, (CY, 32), 0)).astype(F32)
    cell_x = ((cells >> 4) == lax.broadcasted_iota(jnp.int32, (CX, 32), 0)).astype(F32)
    lane_x = lax.broadcasted_iota(jnp.int32, (CX, NZ), 1) >> 3
    lane_q = lax.broadcasted_iota(jnp.int32, (8, NZ), 1) & 7
    at_x = dot(cell_x, (lane_x == lax.broadcasted_iota(jnp.int32, (CX, NZ), 0)).astype(F32), 0, 0)
    target = dot(
        observed[...], (lane_q == lax.broadcasted_iota(jnp.int32, (8, NZ), 0)).astype(F32), 0, 0
    )
    copies = [pltpu.make_async_copy(coef, coef_out, sem.at[STEPS])]
    copies[0].start()
    for step in range(STEPS):
        sweep(step, gx, elec, mag, coef, tools)
        stored[step] = elec[:, HALO : HALO + CX, 0:CY]
        copies.append(pltpu.make_async_copy(stored.at[step], stored_out.at[step], sem.at[step]))
        copies[-1].start()

    at_depth = lane[0:CY] == ZREC
    record = jnp.zeros((CY, NZ), F32)
    for x in range(CX):
        for q in range(8):
            column = jnp.where(at_depth, stored[q // 2, q % 2, x], 0.0)
            record = record + pltpu.roll(column, (x * 8 + q - ZREC) % NZ, 1)
    at_receivers = dot(at_y, record, 0, 0)
    residual = at_x * (at_receivers - target)
    misfit = 0.5 * jnp.sum(residual * residual)
    spread_now = dot(at_y, residual, 1, 0)
    lane8 = lax.broadcasted_iota(jnp.int32, (8, NZ), 1)
    row8 = lax.broadcasted_iota(jnp.int32, (8, NZ), 0)
    spread[...] = spread_now
    low_rows, high_rows = spread_now[0:8], spread_now[8:16]
    edges = jnp.where((lane8 < 32) | (lane8 >= 96), low_rows, pltpu.roll(high_rows, 64, 1))
    is_first = gy == 0
    side = jnp.where(is_first, high_rows, low_rows)
    used = row8 // HALO == 1 - gy
    side = jnp.where(used, side, misfit)
    for t in range(16):
        block[t, 0:8] = edges
        block[t, 8:16] = side
    for copy in copies:
        copy.wait()


def adjoint_kernel(adj, from_prev, from_next, from_side, coef_in, stored_in, *refs):
    spread, blocks, foot, owner, keep, away = refs[:6]
    coef, stored, elec, mag, inject, grad, sem = refs[6:]
    gx, gy = lax.axis_index("gx"), lax.axis_index("gy")
    tools = helpers(gy)
    lane, inside = tools[0], tools[1]

    copies = [
        pltpu.make_async_copy(adj.at[0, 0:3], elec.at[:, HALO : HALO + CX, 0:CY], sem.at[0]),
        pltpu.make_async_copy(adj.at[0, 3:6], mag.at[:, HALO : HALO + CX, 0:CY], sem.at[1]),
        pltpu.make_async_copy(coef_in, coef, sem.at[2]),
    ] + [
        pltpu.make_async_copy(stored_in.at[k], stored.at[k], sem.at[3 + k])
        for k in reversed(range(STEPS))
    ]
    for copy in copies:
        copy.start()
    zero_rows = jnp.zeros((HALO, NZ), F32)
    zero_plane = jnp.zeros((EY, NZ), F32)
    targets = [(elec, c) for c in range(3)] + [(mag, c) for c in range(3)]
    for c, (ref, index) in enumerate(targets):
        filled = set(range(HALO, HALO + CX))
        for source, planes, base in (
            (from_prev, ADJ_LOW, HALO - CX),
            (from_next, ADJ_HIGH, HALO + CX),
        ):
            for k, (comp, x) in enumerate(planes):
                if comp == c:
                    ref[index, x + base, 0:CY] = source[k]
                    filled.add(x + base)
        for i in range(EXP):
            if i not in filled:
                ref[index, i] = zero_plane

    row8 = lax.broadcasted_iota(jnp.int32, (8, NZ), 0)
    used = row8 // HALO == gy
    for k, dx in enumerate((-1, 0, 1)):
        there = (gx + dx >= 0) & (gx + dx < 8)
        near = jnp.clip(gx + dx, 0, 7)
        if dx == 0:
            inject[k, 0:16] = spread[...]
        else:
            edges = jnp.where(there, blocks[2 * near + gy, 0:8], 0.0)
            inject[k, 0:8] = edges
            inject[k, 8:16] = pltpu.roll(edges, 64, 1)
        side = blocks[2 * near + 1 - gy, 8:16]
        inject[k, 16:24] = jnp.where(used & there, side, 0.0)

    first = gy == 0
    for c, (ref, index) in enumerate(targets):
        for i in range(EX):
            rows = from_side[c, i]
            ref[index, i, CY : CY + HALO] = jnp.where(first, rows, zero_rows)
            ref[index, i, CY + HALO : EY] = jnp.where(first, zero_rows, rows)
    for copy in copies[:3]:
        copy.wait()

    at_depth = lane == ZREC

    for step in range(STEPS):
        when = STEPS - 1 - step

        for i in range(step, EX - step):
            source = inject[0 if i < HALO else 1 if i < HALO + CX else 2]
            x = (i - HALO) % CX
            for c in range(2):
                moved = pltpu.roll(source, (ZREC - (x * 8 + 2 * when + c)) % NZ, 1)
                elec[c, i] += jnp.where(at_depth, moved, 0.0)
        sweep(step, gx, elec, mag, coef, tools)

        copies[3 + step].wait()
        for x in range(CX):
            ax, ay, az = (elec[c, HALO + x, 0:CY] for c in range(3))
            horizontal = ax * stored[when, 0, x] + ay * stored[when, 1, x]
            vertical = az * stored[when, 2, x]
            if step:
                horizontal = grad[0, x] + horizontal
                vertical = grad[1, x] + vertical
            grad[0, x] = horizontal
            grad[1, x] = vertical

    flag = foot[0].astype(F32)
    misfit = blocks[0, 8:16][0:1]
    for t in range(1, 16):
        top = 0 if t % 2 == 0 else HALO
        misfit = misfit + blocks[t, 8:16][top : top + 1]
    core = lax.axis_index("tx") & 1
    for z in range(8):
        for ref, mine in ((keep, core), (away, 1 - core)):
            row = owner[2 * z + mine]
            ref[32 * z : 32 * z + 16] = grad[0, row] * flag
            ref[32 * z + 16 : 32 * z + 32] = grad[1, row] * flag
    keep[256:264] = jnp.broadcast_to(misfit, (8, NZ))
    away[256:264] = jnp.broadcast_to(misfit, (8, NZ))


def pair_kernel(mine, other, out):
    misfit = mine[256:264] + other[256:264]
    for z in range(8):
        out[z, 0:32] = mine[32 * z : 32 * z + 32] + other[32 * z : 32 * z + 32]
        out[z, 32:40] = misfit


def sum_kernel(blocks, part, misfit):
    total = blocks[0]
    for z in range(1, 8):
        total = total + blocks[z]
    part[0, 0, 0, 0] = total[0:16]
    part[0, 0, 1, 0] = total[16:32]
    misfit[...] = total[32:33, 0:1]


def on_device(cond_h, cond_v, fwd_init, adj_init, observed, footprint, owner, rec_cells):
    to_next, to_prev, to_side, side_next, side_prev = pack(fwd_init, cond_h, cond_v)
    adj_next, adj_prev = pack_adjoint(adj_init)
    halos = (
        send(to_next, 1, False),
        send(to_prev, -1, False),
        send(to_side, 0, True),
        send(side_next, 1, True),
        send(side_prev, -1, True),
    )
    adj_halos = (send(adj_next, 1, False), send(adj_prev, -1, False))
    coef, stored, spread, block = pl.pallas_call(
        forward_kernel,
        out_shape=[
            pltpu.HBM((4, EXP, EY, NZ), F32),
            pltpu.HBM((STEPS, 3, CX, CY, NZ), F32),
            shape(CY, NZ),
            shape(16, 16, NZ),
        ],
        in_specs=[VMEM] * 10,
        out_specs=[HBM, HBM, VMEM, VMEM],
        scratch_shapes=[
            pltpu.VMEM((4, EXP, EY, NZ), F32),
            pltpu.VMEM((STEPS, 3, CX, CY, NZ), F32),
            pltpu.VMEM((3, EXP, EY, NZ), F32),
            pltpu.VMEM((3, EXP, EY, NZ), F32),
            pltpu.SemaphoreType.DMA((STEPS + 1,)),
        ],
        compiler_params=params(),
        name="forward",
    )(fwd_init, cond_h, cond_v, *halos, observed.reshape(8, 32), rec_cells.reshape(1, 32))
    block, *adj_ready = lax.optimization_barrier((block, *adj_halos))
    adj_side = pl.pallas_call(
        pack_side_kernel,
        out_shape=shape(6, EX, HALO, NZ),
        in_specs=[VMEM] * 3,
        out_specs=VMEM,
        compiler_params=params(),
        name="pack_side",
    )(adj_init, *adj_ready)
    from_side = send(adj_side, 0, True)
    blocks = lax.all_to_all(block, ("gx", "gy"), 0, 0, tiled=True)
    keep, away = pl.pallas_call(
        adjoint_kernel,
        out_shape=[shape(264, NZ)] * 2,
        in_specs=[HBM] + [VMEM] * 3 + [HBM] * 2 + [VMEM] * 2 + [SMEM, SMEM],
        out_specs=[VMEM] * 2,
        scratch_shapes=[
            pltpu.VMEM((4, EXP, EY, NZ), F32),
            pltpu.VMEM((STEPS, 3, CX, CY, NZ), F32),
            pltpu.VMEM((3, EXP, EY, NZ), F32),
            pltpu.VMEM((3, EXP, EY, NZ), F32),
            pltpu.VMEM((3, EY, NZ), F32),
            pltpu.VMEM((2, CX, CY, NZ), F32),
            pltpu.SemaphoreType.DMA((3 + STEPS,)),
        ],
        compiler_params=params(),
        name="adjoint",
    )(
        in_hbm(adj_init),
        *adj_halos,
        from_side,
        in_hbm(coef),
        in_hbm(stored),
        spread,
        blocks,
        footprint.reshape(1),
        owner.reshape(16),
    )
    size = lax.axis_size("tx")
    other = lax.ppermute(away, "tx", [(t, t ^ 1) for t in range(size)])
    paired = pl.pallas_call(
        pair_kernel,
        out_shape=shape(8, 40, NZ),
        in_specs=[VMEM] * 2,
        out_specs=VMEM,
        compiler_params=params(),
        name="pair",
    )(keep, other)
    along_z = [list(range(core, size, 2)) for core in range(2)]
    summed = lax.all_to_all(paired, "tx", 0, 0, axis_index_groups=along_z, tiled=True)
    part, misfit = pl.pallas_call(
        sum_kernel,
        out_shape=[shape(1, 1, 2, 1, CY, NZ), shape(1, 1)],
        in_specs=[VMEM],
        out_specs=[VMEM, VMEM],
        compiler_params=params(),
        name="total",
    )(summed)
    return part, misfit.reshape(())


def solution(mesh):
    placed = (
        P("gx", "gy", None),
        P("gx", "gy", None),
        P("tx", None, "gx", "gy", None),
        P("tx", None, "gx", "gy", None),
        P("tx", None, "gx", "gy", None, None),
        P("tx", "gx", "gy"),
        P("gx", "gy", None),
        P("gx", "gy", None),
    )
    return jax.shard_map(
        on_device,
        mesh=mesh,
        in_specs=placed,
        out_specs=(P("gx", "tx", None, None, "gy", None), P()),
        check_vma=False,
    )
```

```python
import jax
import jax.numpy as jnp
from jax import lax
from jax.experimental import pallas as pl
from jax.experimental.pallas import tpu as pltpu
from jax.sharding import PartitionSpec as P

STEPS = 4
ZREC = 32
STEP_DT = 0.5
HALO = 4
CX = 16
CY = 16
NZ = 128
EX = CX + 2 * HALO
EXP = EX + 4
EY = CY + 2 * HALO
F32 = jnp.float32
HIGHEST = lax.Precision.HIGHEST

LOW = [(c, x) for c in range(8) for x in range(CX - HALO + (c in (3, 6, 7)), CX)]
HIGH = [(c, x) for c in range(8) for x in range(HALO - (c not in (1, 2)))]
ADJ_LOW = [(c, x) for c, x in LOW if c < 6]
ADJ_HIGH = [(c, x) for c, x in HIGH if c < 6]
VMEM = pl.BlockSpec(memory_space=pltpu.VMEM)
SMEM = pl.BlockSpec(memory_space=pltpu.SMEM)
HBM = pl.BlockSpec(memory_space=pltpu.HBM)


def shape(*dims):
    return jax.ShapeDtypeStruct(dims, F32)


def in_hbm(array):
    return pltpu.with_memory_space_constraint(array, pltpu.HBM)


def params():
    return pltpu.CompilerParams(vmem_limit_bytes=8 * 1024 * 1024)


def plane_of(refs, comp, x):
    return refs[0][0, comp, x] if comp < 6 else refs[comp - 5][x]


def edge_of(plane, second):
    return jnp.where(second, plane[0:HALO], plane[CY - HALO : CY])


def pack_adjoint_kernel(adj, to_next, to_prev, sem):
    copies = []
    for ref, planes in ((to_next, ADJ_LOW), (to_prev, ADJ_HIGH)):
        for c in range(6):
            ks = [k for k, (comp, _) in enumerate(planes) if comp == c]
            x = planes[ks[0]][1]
            src, dst = adj.at[0, c, x : x + len(ks)], ref.at[ks[0] : ks[-1] + 1]
            copies.append(pltpu.make_async_copy(src, dst, sem.at[len(copies)]))
    for copy in copies:
        copy.start()
    for copy in copies:
        copy.wait()


def pack_adjoint(adj):
    return pl.pallas_call(
        pack_adjoint_kernel,
        out_shape=[shape(len(ADJ_LOW), CY, NZ), shape(len(ADJ_HIGH), CY, NZ)],
        in_specs=[HBM],
        out_specs=[VMEM] * 2,
        scratch_shapes=[pltpu.SemaphoreType.DMA((12,))],
        compiler_params=params(),
        name="pack_adjoint",
    )(in_hbm(adj))


def pack_kernel(fwd, cond_h, cond_v, *refs):
    to_next, to_prev, to_side, side_next, side_prev = refs[:5]
    bufs, sem = refs[5:8], refs[8]
    moves = [(fwd.at[0, 0:3], bufs[0].at[0, 0:3]), (fwd.at[0, 3:6], bufs[0].at[0, 3:6])]
    moves += [(cond_h, bufs[1]), (cond_v, bufs[2])]
    copies = [
        pltpu.make_async_copy(src, dst, sem.at[k]) for k, (src, dst) in enumerate(moves)
    ]
    for copy in copies:
        copy.start()
    second = lax.axis_index("gy") == 1
    for which, comps in ((0, range(3)), (1, range(3, 6)), (2, (6,)), (3, (7,))):
        copies[which].wait()
        for c in comps:
            edges = [edge_of(plane_of(bufs, c, x), second) for x in range(CX)]
            for x in range(CX):
                to_side[c, x] = edges[x]
            for k, (comp, x) in enumerate(LOW):
                if comp == c:
                    to_next[k] = plane_of(bufs, c, x)
                    side_next[k] = edges[x]
            for k, (comp, x) in enumerate(HIGH):
                if comp == c:
                    to_prev[k] = plane_of(bufs, c, x)
                    side_prev[k] = edges[x]


def pack(*arrays):
    return pl.pallas_call(
        pack_kernel,
        out_shape=[
            shape(len(LOW), CY, NZ),
            shape(len(HIGH), CY, NZ),
            shape(8, CX, HALO, NZ),
            shape(len(LOW), HALO, NZ),
            shape(len(HIGH), HALO, NZ),
        ],
        in_specs=[HBM] * 3,
        out_specs=[VMEM] * 5,
        scratch_shapes=[pltpu.VMEM(a.shape, F32) for a in arrays]
        + [pltpu.SemaphoreType.DMA((4,))],
        compiler_params=params(),
        name="pack",
    )(*(in_hbm(a) for a in arrays))


def pack_side_kernel(adj, from_prev, from_next, to_side):
    second = lax.axis_index("gy") == 1
    for c in range(6):
        for x in range(CX):
            to_side[c, HALO + x] = edge_of(adj[0, c, x], second)
        filled = set(range(HALO, HALO + CX))
        for k, (comp, x) in enumerate(ADJ_LOW):
            if comp == c:
                to_side[c, x - (CX - HALO)] = edge_of(from_prev[k], second)
                filled.add(x - (CX - HALO))
        for k, (comp, x) in enumerate(ADJ_HIGH):
            if comp == c:
                to_side[c, x + HALO + CX] = edge_of(from_next[k], second)
                filled.add(x + HALO + CX)
        for i in range(EX):
            if i not in filled:
                to_side[c, i] = jnp.zeros((HALO, NZ), F32)


def pairs(dx, swap):
    size_x = lax.axis_size("gx")
    size_y = lax.axis_size("gy")
    return [
        (x * size_y + y, (x + dx) * size_y + (1 - y if swap else y))
        for x in range(size_x)
        for y in range(size_y)
        if 0 <= x + dx < size_x
    ]


def send(array, dx, swap):
    return lax.ppermute(array, ("gx", "gy"), pairs(dx, swap))


def assemble(own, halos, comps, first):
    from_prev, from_next, from_side, side_prev, side_next = halos
    zero_rows = jnp.zeros((HALO, NZ), F32)
    zero_plane = jnp.zeros((EY, NZ), F32)

    def put(ref, index, i, plane, rows):
        ref[index, i, 0:CY] = plane
        ref[index, i, CY : CY + HALO] = jnp.where(first, rows, zero_rows)
        ref[index, i, CY + HALO : EY] = jnp.where(first, zero_rows, rows)

    for c, (ref, index) in comps.items():
        filled = set()
        for x in range(CX):
            put(ref, index, HALO + x, own(c, x), from_side[c, x])
            filled.add(HALO + x)
        for k, (comp, x) in enumerate(LOW):
            if comp == c:
                i = x - (CX - HALO)
                put(ref, index, i, from_prev[k], side_prev[k])
                filled.add(i)
        for k, (comp, x) in enumerate(HIGH):
            if comp == c:
                i = x + HALO + CX
                put(ref, index, i, from_next[k], side_next[k])
                filled.add(i)
        for i in range(EXP):
            if i not in filled:
                ref[index, i] = zero_plane


def helpers(gy):
    lane = lax.broadcasted_iota(jnp.int32, (EY, NZ), 1)
    row = lax.broadcasted_iota(jnp.int32, (EY, NZ), 0)
    y = jnp.where(row < CY + HALO, row, row - EY) + gy * CY
    inside = (y >= 0) & (y < 2 * CY)
    last, start = lane == NZ - 1, lane == 0

    def z_up(f):
        return jnp.where(last, 0.0, pltpu.roll(f, NZ - 1, 1))

    def z_down(f):
        return jnp.where(start, 0.0, pltpu.roll(f, 1, 1))

    def y_up(f):
        return pltpu.roll(f, EY - 1, 0)

    def y_down(f):
        return pltpu.roll(f, 1, 0)

    return lane, inside, z_up, z_down, y_up, y_down


def in_grid(gx, i):
    x = gx * CX + i - HALO
    return (x >= 0) & (x < 8 * CX)


UNROLL = 24


def sweep(step, gx, elec, mag, coef, tools):
    _, inside, z_up, z_down, y_up, y_down = tools
    half = jnp.where(inside, STEP_DT, 0.0)
    zero = jnp.zeros((EY, NZ), F32)
    count = EX - 1 - 2 * step
    unroll = min(UNROLL, count)
    turns = -(-count // unroll)

    def magnetic(i, field, after):
        ex, ey, ez = field
        _, ey_next, ez_next = after
        rate = jnp.where(in_grid(gx, i), half, zero)
        hx = mag[0, i] - rate * ((y_up(ez) - ez) - (z_up(ey) - ey))
        hy = mag[1, i] - rate * ((z_up(ex) - ex) - (ez_next - ez))
        hz = mag[2, i] - rate * ((ey_next - ey) - (y_up(ex) - ex))
        return hx, hy, hz

    def electric(i, field, now, before):
        ex, ey, ez = field
        hx, hy, hz = now
        decay_h, drive_h, decay_v, drive_v = (coef[k, i] for k in range(4))
        ex = decay_h * ex + drive_h * ((hz - y_down(hz)) - (hy - z_down(hy)))
        ey = decay_h * ey + drive_h * ((hx - z_down(hx)) - (hz - before[2]))
        ez = decay_v * ez + drive_v * ((hy - before[1]) - (hx - y_down(hx)))
        return ex, ey, ez

    def planes(ref, i, n):
        return [tuple(ref[c, i + k] for c in range(3)) for k in range(n)]

    def put(ref, i, values):
        for k, plane in enumerate(values):
            for c in range(3):
                ref[c, i + k] = plane[c]

    def body(turn, carry):
        i = step + turn * unroll
        field = planes(elec, i, unroll + 1)
        now = [magnetic(i + k, field[k], field[k + 1]) for k in range(unroll)]
        put(mag, i, now)
        before = [(None, *carry)] + now[:-1]
        put(elec, i, [electric(i + k, field[k], now[k], before[k]) for k in range(unroll)])
        return now[-1][1:]

    if turns == 1:
        body(0, (zero, zero))
    else:
        lax.fori_loop(0, turns, body, (zero, zero))


def dot(a, b, dim_a, dim_b):
    dims = (((dim_a,), (dim_b,)), ((), ()))
    return lax.dot_general(a, b, dims, precision=HIGHEST, preferred_element_type=F32)


def forward_kernel(fwd, cond_h, cond_v, *refs):
    halos, refs = refs[:5], refs[5:]
    observed, rec_vec, coef_out, stored_out, spread, block = refs[:6]
    coef, stored, elec, mag, sem = refs[6:]
    gx, gy = lax.axis_index("gx"), lax.axis_index("gy")
    tools = helpers(gy)
    lane, inside = tools[0], tools[1]

    comps = {c: (elec, c) if c < 3 else (mag, c - 3) for c in range(6)}
    comps |= {6: (coef, 0), 7: (coef, 2)}
    assemble(lambda c, x: plane_of((fwd, cond_h, cond_v, None), c, x), halos, comps, gy == 0)

    def coefficients(turn, carry):
        for i in [turn * 8 + k for k in range(8)]:
            keep = inside & in_grid(gx, i)
            for k in (0, 2):
                half_rate = 0.25 * coef[k, i]
                inverse = 1.0 / (1.0 + half_rate)
                coef[k, i] = jnp.where(keep, (1.0 - half_rate) * inverse, 0.0)
                coef[k + 1, i] = jnp.where(keep, STEP_DT * inverse, 0.0)
        return carry

    lax.fori_loop(0, EX // 8, coefficients, 0)
    for k in (1, 3):
        coef[k, EX:EXP] = jnp.zeros((EXP - EX, EY, NZ), F32)

    cells = rec_vec[...]
    at_y = ((cells & 15) == lax.broadcasted_iota(jnp.int32, (CY, 32), 0)).astype(F32)
    cell_x = ((cells >> 4) == lax.broadcasted_iota(jnp.int32, (CX, 32), 0)).astype(F32)
    lane_x = lax.broadcasted_iota(jnp.int32, (CX, NZ), 1) >> 3
    lane_q = lax.broadcasted_iota(jnp.int32, (8, NZ), 1) & 7
    at_x = dot(cell_x, (lane_x == lax.broadcasted_iota(jnp.int32, (CX, NZ), 0)).astype(F32), 0, 0)
    target = dot(
        observed[...], (lane_q == lax.broadcasted_iota(jnp.int32, (8, NZ), 0)).astype(F32), 0, 0
    )
    copies = [pltpu.make_async_copy(coef, coef_out, sem.at[STEPS])]
    copies[0].start()
    for step in range(STEPS):
        sweep(step, gx, elec, mag, coef, tools)
        stored[step] = elec[:, HALO : HALO + CX, 0:CY]
        copies.append(pltpu.make_async_copy(stored.at[step], stored_out.at[step], sem.at[step]))
        copies[-1].start()

    at_depth = lane[0:CY] == ZREC
    record = jnp.zeros((CY, NZ), F32)
    for x in range(CX):
        for q in range(8):
            column = jnp.where(at_depth, stored[q // 2, q % 2, x], 0.0)
            record = record + pltpu.roll(column, (x * 8 + q - ZREC) % NZ, 1)
    at_receivers = dot(at_y, record, 0, 0)
    residual = at_x * (at_receivers - target)
    misfit = 0.5 * jnp.sum(residual * residual)
    spread_now = dot(at_y, residual, 1, 0)
    lane8 = lax.broadcasted_iota(jnp.int32, (8, NZ), 1)
    row8 = lax.broadcasted_iota(jnp.int32, (8, NZ), 0)
    spread[...] = spread_now
    low_rows, high_rows = spread_now[0:8], spread_now[8:16]
    edges = jnp.where((lane8 < 32) | (lane8 >= 96), low_rows, pltpu.roll(high_rows, 64, 1))
    is_first = gy == 0
    side = jnp.where(is_first, high_rows, low_rows)
    used = row8 // HALO == 1 - gy
    side = jnp.where(used, side, misfit)
    for t in range(16):
        block[t, 0:8] = edges
        block[t, 8:16] = side
    for copy in copies:
        copy.wait()


def adjoint_kernel(adj, from_prev, from_next, from_side, coef_in, stored_in, *refs):
    spread, blocks, foot, owner, keep, away = refs[:6]
    coef, stored, elec, mag, inject, grad, sem = refs[6:]
    gx, gy = lax.axis_index("gx"), lax.axis_index("gy")
    tools = helpers(gy)
    lane, inside = tools[0], tools[1]

    copies = [
        pltpu.make_async_copy(adj.at[0, 0:3], elec.at[:, HALO : HALO + CX, 0:CY], sem.at[0]),
        pltpu.make_async_copy(adj.at[0, 3:6], mag.at[:, HALO : HALO + CX, 0:CY], sem.at[1]),
        pltpu.make_async_copy(coef_in, coef, sem.at[2]),
    ] + [
        pltpu.make_async_copy(stored_in.at[k], stored.at[k], sem.at[3 + k])
        for k in reversed(range(STEPS))
    ]
    for copy in copies:
        copy.start()
    zero_rows = jnp.zeros((HALO, NZ), F32)
    zero_plane = jnp.zeros((EY, NZ), F32)
    targets = [(elec, c) for c in range(3)] + [(mag, c) for c in range(3)]
    for c, (ref, index) in enumerate(targets):
        filled = set(range(HALO, HALO + CX))
        for source, planes, base in (
            (from_prev, ADJ_LOW, HALO - CX),
            (from_next, ADJ_HIGH, HALO + CX),
        ):
            for k, (comp, x) in enumerate(planes):
                if comp == c:
                    ref[index, x + base, 0:CY] = source[k]
                    filled.add(x + base)
        for i in range(EXP):
            if i not in filled:
                ref[index, i] = zero_plane

    row8 = lax.broadcasted_iota(jnp.int32, (8, NZ), 0)
    used = row8 // HALO == gy
    for k, dx in enumerate((-1, 0, 1)):
        there = (gx + dx >= 0) & (gx + dx < 8)
        near = jnp.clip(gx + dx, 0, 7)
        if dx == 0:
            inject[k, 0:16] = spread[...]
        else:
            edges = jnp.where(there, blocks[2 * near + gy, 0:8], 0.0)
            inject[k, 0:8] = edges
            inject[k, 8:16] = pltpu.roll(edges, 64, 1)
        side = blocks[2 * near + 1 - gy, 8:16]
        inject[k, 16:24] = jnp.where(used & there, side, 0.0)

    first = gy == 0
    for c, (ref, index) in enumerate(targets):
        for i in range(EX):
            rows = from_side[c, i]
            ref[index, i, CY : CY + HALO] = jnp.where(first, rows, zero_rows)
            ref[index, i, CY + HALO : EY] = jnp.where(first, zero_rows, rows)
    copies[0].wait()
    at_depth = lane == ZREC

    for step in range(STEPS):
        when = STEPS - 1 - step

        for i in range(step, EX - step):
            source = inject[0 if i < HALO else 1 if i < HALO + CX else 2]
            x = (i - HALO) % CX
            for c in range(2):
                moved = pltpu.roll(source, (ZREC - (x * 8 + 2 * when + c)) % NZ, 1)
                elec[c, i] += jnp.where(at_depth, moved, 0.0)
        if step == 0:
            copies[1].wait()
            copies[2].wait()
        sweep(step, gx, elec, mag, coef, tools)

        copies[3 + step].wait()
        for x in range(CX):
            ax, ay, az = (elec[c, HALO + x, 0:CY] for c in range(3))
            horizontal = ax * stored[when, 0, x] + ay * stored[when, 1, x]
            vertical = az * stored[when, 2, x]
            if step:
                horizontal = grad[0, x] + horizontal
                vertical = grad[1, x] + vertical
            grad[0, x] = horizontal
            grad[1, x] = vertical

    flag = foot[0].astype(F32)
    misfit = blocks[0, 8:16][0:1]
    for t in range(1, 16):
        top = 0 if t % 2 == 0 else HALO
        misfit = misfit + blocks[t, 8:16][top : top + 1]
    core = lax.axis_index("tx") & 1
    for z in range(8):
        for ref, mine in ((keep, core), (away, 1 - core)):
            row = owner[2 * z + mine]
            ref[32 * z : 32 * z + 16] = grad[0, row] * flag
            ref[32 * z + 16 : 32 * z + 32] = grad[1, row] * flag
    keep[256:264] = jnp.broadcast_to(misfit, (8, NZ))
    away[256:264] = jnp.broadcast_to(misfit, (8, NZ))


def pair_kernel(mine, other, out):
    misfit = mine[256:264] + other[256:264]
    for z in range(8):
        out[z, 0:32] = mine[32 * z : 32 * z + 32] + other[32 * z : 32 * z + 32]
        out[z, 32:40] = misfit


def sum_kernel(blocks, part, misfit):
    total = blocks[0]
    for z in range(1, 8):
        total = total + blocks[z]
    part[0, 0, 0, 0] = total[0:16]
    part[0, 0, 1, 0] = total[16:32]
    misfit[...] = total[32:33, 0:1]


def on_device(cond_h, cond_v, fwd_init, adj_init, observed, footprint, owner, rec_cells):
    to_next, to_prev, to_side, side_next, side_prev = pack(fwd_init, cond_h, cond_v)
    adj_next, adj_prev = pack_adjoint(adj_init)
    halos = (
        send(to_next, 1, False),
        send(to_prev, -1, False),
        send(to_side, 0, True),
        send(side_next, 1, True),
        send(side_prev, -1, True),
    )
    adj_halos = (send(adj_next, 1, False), send(adj_prev, -1, False))
    coef, stored, spread, block = pl.pallas_call(
        forward_kernel,
        out_shape=[
            pltpu.HBM((4, EXP, EY, NZ), F32),
            pltpu.HBM((STEPS, 3, CX, CY, NZ), F32),
            shape(CY, NZ),
            shape(16, 16, NZ),
        ],
        in_specs=[VMEM] * 10,
        out_specs=[HBM, HBM, VMEM, VMEM],
        scratch_shapes=[
            pltpu.VMEM((4, EXP, EY, NZ), F32),
            pltpu.VMEM((STEPS, 3, CX, CY, NZ), F32),
            pltpu.VMEM((3, EXP, EY, NZ), F32),
            pltpu.VMEM((3, EXP, EY, NZ), F32),
            pltpu.SemaphoreType.DMA((STEPS + 1,)),
        ],
        compiler_params=params(),
        name="forward",
    )(fwd_init, cond_h, cond_v, *halos, observed.reshape(8, 32), rec_cells.reshape(1, 32))
    block, *adj_ready = lax.optimization_barrier((block, *adj_halos))
    adj_side = pl.pallas_call(
        pack_side_kernel,
        out_shape=shape(6, EX, HALO, NZ),
        in_specs=[VMEM] * 3,
        out_specs=VMEM,
        compiler_params=params(),
        name="pack_side",
    )(adj_init, *adj_ready)
    from_side = send(adj_side, 0, True)
    blocks = lax.all_to_all(block, ("gx", "gy"), 0, 0, tiled=True)
    keep, away = pl.pallas_call(
        adjoint_kernel,
        out_shape=[shape(264, NZ)] * 2,
        in_specs=[HBM] + [VMEM] * 3 + [HBM] * 2 + [VMEM] * 2 + [SMEM, SMEM],
        out_specs=[VMEM] * 2,
        scratch_shapes=[
            pltpu.VMEM((4, EXP, EY, NZ), F32),
            pltpu.VMEM((STEPS, 3, CX, CY, NZ), F32),
            pltpu.VMEM((3, EXP, EY, NZ), F32),
            pltpu.VMEM((3, EXP, EY, NZ), F32),
            pltpu.VMEM((3, EY, NZ), F32),
            pltpu.VMEM((2, CX, CY, NZ), F32),
            pltpu.SemaphoreType.DMA((3 + STEPS,)),
        ],
        compiler_params=params(),
        name="adjoint",
    )(
        in_hbm(adj_init),
        *adj_halos,
        from_side,
        in_hbm(coef),
        in_hbm(stored),
        spread,
        blocks,
        footprint.reshape(1),
        owner.reshape(16),
    )
    size = lax.axis_size("tx")
    other = lax.ppermute(away, "tx", [(t, t ^ 1) for t in range(size)])
    paired = pl.pallas_call(
        pair_kernel,
        out_shape=shape(8, 40, NZ),
        in_specs=[VMEM] * 2,
        out_specs=VMEM,
        compiler_params=params(),
        name="pair",
    )(keep, other)
    along_z = [list(range(core, size, 2)) for core in range(2)]
    summed = lax.all_to_all(paired, "tx", 0, 0, axis_index_groups=along_z, tiled=True)
    part, misfit = pl.pallas_call(
        sum_kernel,
        out_shape=[shape(1, 1, 2, 1, CY, NZ), shape(1, 1)],
        in_specs=[VMEM],
        out_specs=[VMEM, VMEM],
        compiler_params=params(),
        name="total",
    )(summed)
    return part, misfit.reshape(())


def solution(mesh):
    placed = (
        P("gx", "gy", None),
        P("gx", "gy", None),
        P("tx", None, "gx", "gy", None),
        P("tx", None, "gx", "gy", None),
        P("tx", None, "gx", "gy", None, None),
        P("tx", "gx", "gy"),
        P("gx", "gy", None),
        P("gx", "gy", None),
    )
    return jax.shard_map(
        on_device,
        mesh=mesh,
        in_specs=placed,
        out_specs=(P("gx", "tx", None, None, "gy", None), P()),
        check_vma=False,
    )
```
